512 devices in a mesh: dp: 64 (over z, y_hi, core), sub: 8 (over y_lo, x).
Axes of the slice: x: 4, y: 8 (y_hi: 4, y_lo: 2; y = y_hi * 2 + y_lo), z: 8, core: 2. Of those that a mesh axis runs over, the one named last changes fastest.
Arguments:
- activations: bfloat16 [1024, 14, 14, 384], P(('dp', 'sub')), may hold values from -6 to 6
- cotangent: bfloat16 [1024, 14, 14, 384], P(('dp', 'sub')), may hold values from -0.29882812 to 0.29882812
- kernel: bfloat16 [384, 1152], replicated, may hold values from -0.1875 to 0.1875
- channel_gain: float32 [384], replicated, may hold values from 0.5 to 4
- master_flat: float32 [442368], P(('dp', 'sub')), may hold values from -6 to 6
- moment_mean: float32 [442368], P(('dp', 'sub')), may hold values from -9.408 to 9.408
- moment_square: float32 [442368], P(('dp', 'sub')), may hold values from 0.0401408 to 1.00352
Outputs:
- input_grad: bfloat16 [1024, 14, 14, 384], P(('dp', 'sub'))
- master_next: float32 [442368], P(('dp', 'sub'))
- mean_next: float32 [442368], P(('dp', 'sub'))
- square_next: float32 [442368], P(('dp', 'sub'))
- kernel_next: bfloat16 [384, 1152], replicated
The draws below stay inside these ranges and needn't reach their ends.
All inputs are finite; a program needn't handle non-finite values.
Results may differ from the reference program's by a relative error of at most 0.006.
Values may be sent and summed in bfloat16 or wider, within the bound.
No kernel may reach another device: no remote copies, remote signals or barrier semaphores. Data moves between devices by JAX's collectives and lax.ppermute only.
A program may use at most 64 MiB of HBM per device.

```python
import math
import jax
import jax.numpy as jnp
from jax import lax

CMID = 384
CG = 128
SIDE = 14
IMG_DEV = 2
ADAM_STEP = 10
GROUPS = 3
FAN = 1152
IMAGES = 1024


def draw_master_flat(key, part):
    subkeys = jax.random.split(jax.random.fold_in(key, 17), 3)
    row_scale = jnp.exp(jax.random.uniform(subkeys[0], (CMID, 1), jnp.float32, math.log(0.3), math.log(3.0)))
    col_scale = jnp.exp(jax.random.uniform(subkeys[1], (1, FAN), jnp.float32, math.log(0.3), math.log(3.0)))
    entries = jax.random.normal(subkeys[2], (CMID, FAN), jnp.float32)
    return jnp.clip(0.12 * row_scale * col_scale * entries, -6.0, 6.0).reshape(CMID * FAN)


def levels(key, extent, cuts, least, largest):
    level, own = 1.0, jax.random.fold_in(key, 6)
    for dim, blocks in cuts:
        heights = jnp.exp(jax.random.uniform(jax.random.fold_in(own, dim), (blocks,), jnp.float32, least / len(cuts), largest / len(cuts)))
        level = level * jnp.repeat(heights, extent[dim] // blocks).reshape([-1 if axis == dim else 1 for axis in range(len(extent))])
    return level


def centred(key, extent, spread, limit, shards=(), kind=jnp.bfloat16):
    result = jax.random.normal(key, extent, jnp.float32) * spread
    if len(shards) > 0:
        result = levels(key, extent, shards, -0.22, 0.18) * result
    return jnp.clip(result, min=-limit, max=limit).astype(kind)


def setup_inputs(seed: int = 0) -> dict:
    splits = jax.random.split(jax.random.key(seed), 8)
    return {
        "activations": centred(splits[0], (IMAGES, SIDE, SIDE, CMID), 1.0, 6.0, ((0, 512),)),
        "cotangent": centred(splits[1], (IMAGES, SIDE, SIDE, CMID), 0.05, 0.29882812, ((0, 512),)),
        "kernel": centred(splits[2], (CMID, FAN), FAN ** -0.5, 0.1875),
        "channel_gain": jnp.clip(jnp.exp(jax.random.uniform(splits[3], (CMID,), jnp.float32, math.log(0.5), math.log(4.0))), 0.5, 4.0),
        "master_flat": draw_master_flat(jax.random.fold_in(splits[7], 71), 0),
        "moment_mean": centred(splits[5], (CMID * FAN,), (0.0035 * (IMAGES * SIDE * SIDE) ** 0.5), 9.408, ((0, 512),), jnp.float32),
        "moment_square": jnp.clip(jnp.exp(math.log(1.00352) - 3.218876 * jax.random.uniform(splits[6], (CMID * FAN,), jnp.float32) ** levels(splits[6], (CMID * FAN,), ((0, 512),), -0.2, 0.2)), 0.0401408, 1.00352),
    }


HALF_ROOT = 0.7071067811865476
INV_ROOT_TAU = 0.3989422804014327

def gelu_slope(values):
    return 0.5 * (1.0 + lax.erf(values * HALF_ROOT)) + values * jnp.exp(-0.5 * values * values) * INV_ROOT_TAU

def forward(images, kernel_taps):
    batch, side = (images.shape[0], images.shape[1])
    padded = jnp.pad(images.astype(jnp.float32), ((0, 0), (1, 1), (1, 1), (0, 0))).reshape(batch, side + 2, side + 2, GROUPS, CG)
    total = jnp.zeros((batch, side, side, GROUPS, CG), jnp.float32)
    for tap_index in range(9):
        row_off, col_off = (tap_index // 3, tap_index % 3)
        window = padded[:, row_off:row_off + side, col_off:col_off + side]
        total = total + jnp.einsum('bhwgc,gdc->bhwgd', window, kernel_taps[:, :, tap_index, :])
    return total.reshape(batch, side, side, GROUPS * CG)

def input_back(pre_grad, kernel_taps):
    batch, side = (pre_grad.shape[0], pre_grad.shape[1])
    padded = jnp.pad(pre_grad.astype(jnp.float32), ((0, 0), (1, 1), (1, 1), (0, 0))).reshape(batch, side + 2, side + 2, GROUPS, CG)
    total = jnp.zeros((batch, side, side, GROUPS, CG), jnp.float32)
    for tap_index in range(9):
        row_off, col_off = (tap_index // 3, tap_index % 3)
        window = padded[:, 2 - row_off:2 - row_off + side, 2 - col_off:2 - col_off + side]
        total = total + jnp.einsum('bhwgd,gdc->bhwgc', window, kernel_taps[:, :, tap_index, :])
    return total.reshape(batch, side, side, GROUPS * CG)

def kernel_back(images, pre_grad):
    batch, side = (images.shape[0], images.shape[1])
    padded = jnp.pad(images.astype(jnp.float32), ((0, 0), (1, 1), (1, 1), (0, 0))).reshape(batch, side + 2, side + 2, GROUPS, CG)
    upstream = pre_grad.astype(jnp.float32).reshape(batch, side, side, GROUPS, CG)
    terms = []
    for tap_index in range(9):
        row_off, col_off = (tap_index // 3, tap_index % 3)
        window = padded[:, row_off:row_off + side, col_off:col_off + side]
        terms.append(jnp.einsum('bhwgc,bhwgd->gdc', window, upstream))
    return jnp.stack(terms, axis=2).reshape(GROUPS * CG, 9 * CG)

def reference(activations, cotangent, kernel, channel_gain, master_flat, moment_mean, moment_square):
    kernel_taps = kernel.astype(jnp.float32).reshape(GROUPS, CG, 9, CG)
    blocks = IMAGES // IMG_DEV
    image_blocks = activations.reshape(blocks, IMG_DEV, SIDE, SIDE, CMID)
    cot_blocks = cotangent.reshape(blocks, IMG_DEV, SIDE, SIDE, CMID)

    def scan_step(total, inputs_pair):
        images, upstream = inputs_pair
        preact = forward(images, kernel_taps)
        pre_grad = (upstream.astype(jnp.float32) * gelu_slope(preact)).astype(jnp.bfloat16)
        back = input_back(pre_grad, kernel_taps).astype(jnp.bfloat16)
        return (total + kernel_back(images, pre_grad), back)
    grad_full, back_blocks = lax.scan(scan_step, jnp.zeros((CMID, FAN), jnp.float32), (image_blocks, cot_blocks))
    input_grad = back_blocks.reshape(IMAGES, SIDE, SIDE, CMID)
    grad_full = grad_full.reshape(CMID * FAN)
    mean_next = 0.9 * moment_mean + 0.1 * grad_full
    square_next = 0.999 * moment_square + 0.001 * grad_full * grad_full
    fix_mean = 1.0 - 0.9 ** ADAM_STEP
    fix_square = 1.0 - 0.999 ** ADAM_STEP
    update = mean_next / fix_mean / (jnp.sqrt(square_next / fix_square) + 1e-08)
    master_next = master_flat - 0.02 * update
    matrix = master_next.reshape(CMID, FAN)
    chan_mean = lax.optimization_barrier(jnp.sum(matrix, axis=1)) / FAN
    chan_var = lax.optimization_barrier(jnp.sum(matrix * matrix, axis=1)) / FAN - chan_mean * chan_mean
    chan_scale = channel_gain / jnp.sqrt(FAN * chan_var + 0.0001)
    kernel_next = ((matrix - chan_mean[:, None]) * chan_scale[:, None]).astype(jnp.bfloat16)
    return (input_grad, master_next, mean_next, square_next, kernel_next)
```

```python
import jax
import jax.numpy as jnp
from jax import lax
from jax.experimental import pallas as pl
from jax.experimental.pallas import tpu as pltpu
from jax.sharding import Mesh, PartitionSpec as P

CMID = 384
CG = 128
ADAM_STEP = 10
GROUPS = 3
FAN = 1152
SIDE = 14
SHARD = 864
HALF_ROOT = 0.7071067811865476
INV_ROOT_TAU = 0.3989422804014327
bf16 = jnp.bfloat16
f32 = jnp.float32

AXES = ("z", "yh", "co", "yl", "x")
SIZES = (8, 4, 2, 2, 4)
ZY = ("z", "yh", "yl")
BLOCKS = CMID // 3
USED = 27
ROWS = 32
IMG = 256
OUT = SIDE * 16
VMEM = pl.BlockSpec(memory_space=pltpu.VMEM)
SMEM = pl.BlockSpec(memory_space=pltpu.SMEM)


def gelu_slope(values):
    return (
        0.5 * (1.0 + lax.erf(values * HALF_ROOT))
        + values * jnp.exp(-0.5 * values * values) * INV_ROOT_TAU
    )


def shift_columns(full, shifted):
    shifted[0] = pltpu.roll(full, 1, 0).astype(bf16)
    shifted[1] = full.astype(bf16)
    shifted[2] = pltpu.roll(full, full.shape[0] - 1, 0).astype(bf16)


def window(shifted, cols, row_off, col_off):
    return jnp.concatenate(
        [shifted[col_off, n * IMG + row_off * 16 : n * IMG + row_off * 16 + OUT, cols] for n in range(2)],
        0,
    )


def grads_kernel(x_ref, cot_ref, k_ref, pg_ref, keep_ref, give_ref, xf, xs, cf, taps, blocks):
    me = lax.axis_index("co")
    xf[...] = jnp.zeros_like(xf)
    cf[...] = jnp.zeros_like(cf)
    for n in range(2):
        for h in range(SIDE):
            at = n * IMG + (h + 1) * 16
            xf[at : at + SIDE, :] = x_ref[n, h].astype(f32)
            at = n * OUT + h * 16
            cf[at : at + SIDE, :] = cot_ref[n, h].astype(f32)
    shift_columns(xf[...], xs)
    pg_ref[...] = jnp.zeros_like(pg_ref)
    for g in range(GROUPS):
        cols = slice(g * CG, (g + 1) * CG)
        patches = jnp.concatenate([window(xs, cols, t // 3, t % 3) for t in range(9)], 1)
        pre = lax.dot_general(
            patches, k_ref[cols, :], (((1,), (1,)), ((), ())), preferred_element_type=f32
        )
        pg = (cf[:, cols] * gelu_slope(pre)).astype(bf16)
        for n in range(2):
            pg_ref[n * IMG + 16 : n * IMG + 16 + OUT, cols] = pg[n * OUT : (n + 1) * OUT]
        grad = lax.dot_general(pg, patches, (((0,), (0,)), ((), ())), preferred_element_type=f32)
        for t in range(9):
            taps[t, cols, :] = grad[:, t * CG : (t + 1) * CG]
    for t in range(9):
        for r in range(3):
            blocks[pl.ds(9 * r + t, BLOCKS, ROWS), :] = taps[t, pl.ds(r, BLOCKS, 3), :]
    for s in range(USED, ROWS):
        blocks[pl.ds(s, BLOCKS, ROWS), :] = jnp.zeros((BLOCKS, CG), f32)
    for q in range(32):
        kept = pl.multiple_of((2 * q + me) * 64, 64)
        given = pl.multiple_of((2 * q + 1 - me) * 64, 64)
        keep_ref[q * 64 : (q + 1) * 64, :] = blocks[pl.ds(kept, 64), :].astype(bf16)
        give_ref[q * 64 : (q + 1) * 64, :] = blocks[pl.ds(given, 64), :].astype(bf16)


def input_kernel(pg_ref, k_ref, out_ref, ps):
    shift_columns(pg_ref[...].astype(f32), ps)
    for g in range(GROUPS):
        cols = slice(g * CG, (g + 1) * CG)
        patches = jnp.concatenate([window(ps, cols, 2 - t // 3, 2 - t % 3) for t in range(9)], 1)
        taps = jnp.concatenate([k_ref[cols, t * CG : (t + 1) * CG] for t in range(9)], 0)
        back = jnp.dot(patches, taps, preferred_element_type=f32).astype(bf16)
        for n in range(2):
            for h in range(SIDE):
                at = n * OUT + h * 16
                out_ref[n, h, :, cols] = back[at : at + SIDE]


def reduce_kernel(part_ref, mean_ref, square_ref, master_ref, out_ref):
    total = part_ref[0:ROWS, :].astype(f32)
    for i in range(1, 64):
        total = total + part_ref[i * ROWS : (i + 1) * ROWS, :].astype(f32)
    for i in range(4):
        out_ref[i, 0:32, :] = total
        out_ref[i, 32:40, :] = mean_ref[...]
        out_ref[i, 40:48, :] = square_ref[...]
        out_ref[i, 48:56, :] = master_ref[...]


def adam(moment_mean, moment_square, master, grad):
    mean_next = 0.9 * moment_mean + 0.1 * grad
    square_next = 0.999 * moment_square + 0.001 * grad * grad
    fix_mean = 1.0 - 0.9**ADAM_STEP
    fix_square = 1.0 - 0.999**ADAM_STEP
    update = mean_next / fix_mean / (jnp.sqrt(square_next / fix_square) + 1e-08)
    return mean_next, square_next, master - 0.02 * update


def adam_kernel(in_ref, gain_ref, grad_ref, send_ref, frame):
    lane = lax.broadcasted_iota(jnp.int32, (8, CG), 1)
    frame[...] = jnp.zeros_like(frame)
    for p in range(4):
        base, shift = divmod(p * SHARD, CG)
        for k in range(3):
            rows = in_ref[p, 32 + 8 * k : 40 + 8 * k, :]
            if shift:
                rows = pltpu.roll(rows, shift, 1)
            frame[k, base : base + 8, :] += jnp.where(lane >= shift, rows, 0.0)
            if shift:
                frame[k, base + 1 : base + 9, :] += jnp.where(lane < shift, rows, 0.0)
    grad = (in_ref[0, 0:32, :] + in_ref[1, 0:32, :]) + (in_ref[2, 0:32, :] + in_ref[3, 0:32, :])
    grad_ref[...] = grad
    master = adam(frame[0, 0:32, :], frame[1, 0:32, :], frame[2, 0:32, :], grad)[2]
    row = lax.broadcasted_iota(jnp.int32, (32, CG), 0)
    block = (lax.axis_index("z") * 4 + lax.axis_index("yh")) * 4 + lax.axis_index("co") * 2 + lax.axis_index("yl")
    mean_of = jnp.zeros((32, CG), f32)
    scale_of = jnp.zeros((32, CG), f32)
    for r in range(3):
        mine = (row >= 9 * r) & (row < 9 * r + 9)
        values = jnp.where(mine, master, 0.0)
        mean = jnp.sum(jnp.sum(values, 0, keepdims=True), 1, keepdims=True) / FAN
        square = jnp.sum(jnp.sum(values * values, 0, keepdims=True), 1, keepdims=True) / FAN
        scale = gain_ref[block * 3 + r] / jnp.sqrt(FAN * (square - mean * mean) + 0.0001)
        mean_of = jnp.where(mine, mean, mean_of)
        scale_of = jnp.where(mine, scale, scale_of)
    out = ((master - mean_of) * scale_of).astype(bf16)
    for i in range(64):
        send_ref[i * ROWS : (i + 1) * ROWS, :] = out


def assemble_kernel(own_ref, got_ref, out_ref, blocks, taps):
    me = lax.axis_index("co")
    for q in range(32):
        kept = pl.multiple_of((2 * q + me) * 64, 64)
        given = pl.multiple_of((2 * q + 1 - me) * 64, 64)
        blocks[pl.ds(kept, 64), :] = own_ref[q * 64 : (q + 1) * 64, :].astype(f32)
        blocks[pl.ds(given, 64), :] = got_ref[q * 64 : (q + 1) * 64, :].astype(f32)
    for t in range(9):
        for r in range(3):
            taps[t, pl.ds(r, BLOCKS, 3), :] = blocks[pl.ds(9 * r + t, BLOCKS, ROWS), :]
    for t in range(9):
        out_ref[:, t * CG : (t + 1) * CG] = taps[t].astype(bf16)


def shape(dims, dtype):
    return jax.ShapeDtypeStruct(dims, dtype)


def swap_cores(x):
    return lax.ppermute(x, "co", [(0, 1), (1, 0)])


def exchange(x, axes):
    return lax.all_to_all(x, axes, 0, 0, tiled=True)


def on_device(
    activations, cotangent, kernel, channel_gain, master_flat, moment_mean, moment_square
):
    pre_grad, keep, give = pl.pallas_call(
        grads_kernel,
        out_shape=(
            shape((2 * IMG, CMID), bf16),
            shape((64 * ROWS, CG), bf16),
            shape((64 * ROWS, CG), bf16),
        ),
        in_specs=[VMEM] * 3,
        out_specs=(VMEM,) * 3,
        scratch_shapes=[
            pltpu.VMEM((2 * IMG, CMID), f32),
            pltpu.VMEM((3, 2 * IMG, CMID), bf16),
            pltpu.VMEM((2 * OUT, CMID), f32),
            pltpu.VMEM((9, CMID, CG), f32),
            pltpu.VMEM((BLOCKS * ROWS, CG), f32),
        ],
        name="grads",
    )(activations, cotangent, kernel)
    got = swap_cores(give)
    input_grad = pl.pallas_call(
        input_kernel,
        out_shape=shape((2, SIDE, SIDE, CMID), bf16),
        in_specs=[VMEM] * 2,
        out_specs=VMEM,
        scratch_shapes=[pltpu.VMEM((3, 2 * IMG, CMID), bf16)],
        name="input_grad",
    )(pre_grad, kernel)
    pair = (keep.astype(f32) + got.astype(f32)).astype(bf16)
    parts = exchange(pair.reshape(64, ROWS, CG), ZY)
    padded = [
        jnp.pad(flat, (0, 1024 - SHARD)).reshape(8, CG)
        for flat in (moment_mean, moment_square, master_flat)
    ]
    payload = pl.pallas_call(
        reduce_kernel,
        out_shape=shape((4, 56, CG), f32),
        in_specs=[VMEM] * 4,
        out_specs=VMEM,
        name="reduce",
    )(parts.reshape(64 * ROWS, CG), *padded)
    gathered = exchange(payload, "x")
    grad, send = pl.pallas_call(
        adam_kernel,
        out_shape=(shape((ROWS, CG), f32), shape((64 * ROWS, CG), bf16)),
        in_specs=[VMEM, SMEM],
        out_specs=(VMEM,) * 2,
        scratch_shapes=[pltpu.VMEM((3, 40, CG), f32)],
        name="adam",
    )(gathered, channel_gain)
    own = exchange(send.reshape(64, ROWS, CG), ZY).reshape(64 * ROWS, CG)
    other = swap_cores(own)
    grad_shard = lax.dynamic_slice(
        grad.reshape(ROWS * CG), (lax.axis_index("x") * SHARD,), (SHARD,)
    )
    mean_next, square_next, master_next = adam(
        moment_mean, moment_square, master_flat, grad_shard
    )
    kernel_next = pl.pallas_call(
        assemble_kernel,
        out_shape=shape((CMID, FAN), bf16),
        in_specs=[VMEM] * 2,
        out_specs=VMEM,
        scratch_shapes=[
            pltpu.VMEM((BLOCKS * ROWS, CG), f32),
            pltpu.VMEM((9, CMID, CG), f32),
        ],
        name="assemble",
    )(own, other)
    return (input_grad, master_next, mean_next, square_next, kernel_next)


def solution(mesh):
    fine = Mesh(mesh.devices.reshape(SIZES), AXES)
    images = P(AXES, None, None, None)
    state = P(AXES)
    return jax.shard_map(
        on_device,
        mesh=fine,
        in_specs=(images, images, P(), P(), state, state, state),
        out_specs=(images, state, state, state, P()),
        check_vma=False,
    )
```

```python
import jax
import jax.numpy as jnp
from jax import lax
from jax.experimental import pallas as pl
from jax.experimental.pallas import tpu as pltpu
from jax.sharding import Mesh, PartitionSpec as P

CMID = 384
CG = 128
ADAM_STEP = 10
GROUPS = 3
FAN = 1152
SIDE = 14
SHARD = 864
HALF_ROOT = 0.7071067811865476
INV_ROOT_TAU = 0.3989422804014327
bf16 = jnp.bfloat16
f32 = jnp.float32

AXES = ("z", "yh", "co", "yl", "x")
SIZES = (8, 4, 2, 2, 4)
ZY = ("z", "yh", "yl")
BLOCKS = CMID // 3
USED = 27
ROWS = 32
IMG = 256
OUT = SIDE * 16
VMEM = pl.BlockSpec(memory_space=pltpu.VMEM)
SMEM = pl.BlockSpec(memory_space=pltpu.SMEM)


def grant(mib):
    return pltpu.CompilerParams(vmem_limit_bytes=mib * 2**20)


def gelu_slope(values):
    return (
        0.5 * (1.0 + lax.erf(values * HALF_ROOT))
        + values * jnp.exp(-0.5 * values * values) * INV_ROOT_TAU
    )


def shift_columns(full, shifted):
    shifted[0] = pltpu.roll(full, 1, 0).astype(bf16)
    shifted[1] = full.astype(bf16)
    shifted[2] = pltpu.roll(full, full.shape[0] - 1, 0).astype(bf16)


def window(shifted, cols, row_off, col_off):
    return jnp.concatenate(
        [shifted[col_off, n * IMG + row_off * 16 : n * IMG + row_off * 16 + OUT, cols] for n in range(2)],
        0,
    )


def grads_kernel(x_ref, cot_ref, k_ref, pg_ref, keep_ref, give_ref, xf, xs, cf, taps, blocks):
    me = lax.axis_index("co")
    xf[...] = jnp.zeros_like(xf)
    cf[...] = jnp.zeros_like(cf)
    for n in range(2):
        for h in range(SIDE):
            at = n * IMG + (h + 1) * 16
            xf[at : at + SIDE, :] = x_ref[n, h].astype(f32)
            at = n * OUT + h * 16
            cf[at : at + SIDE, :] = cot_ref[n, h].astype(f32)
    shift_columns(xf[...], xs)
    pg_ref[...] = jnp.zeros_like(pg_ref)
    for g in range(GROUPS):
        cols = slice(g * CG, (g + 1) * CG)
        patches = jnp.concatenate([window(xs, cols, t // 3, t % 3) for t in range(9)], 1)
        pre = lax.dot_general(
            patches, k_ref[cols, :], (((1,), (1,)), ((), ())), preferred_element_type=f32
        )
        pg = (cf[:, cols] * gelu_slope(pre)).astype(bf16)
        for n in range(2):
            pg_ref[n * IMG + 16 : n * IMG + 16 + OUT, cols] = pg[n * OUT : (n + 1) * OUT]
        grad = lax.dot_general(pg, patches, (((0,), (0,)), ((), ())), preferred_element_type=f32)
        for t in range(9):
            taps[t, cols, :] = grad[:, t * CG : (t + 1) * CG]
    for t in range(9):
        for r in range(3):
            blocks[pl.ds(9 * r + t, BLOCKS, ROWS), :] = taps[t, pl.ds(r, BLOCKS, 3), :]
    for s in range(USED, ROWS):
        blocks[pl.ds(s, BLOCKS, ROWS), :] = jnp.zeros((BLOCKS, CG), f32)
    for q in range(32):
        kept = pl.multiple_of((2 * q + me) * 64, 64)
        given = pl.multiple_of((2 * q + 1 - me) * 64, 64)
        keep_ref[q * 64 : (q + 1) * 64, :] = blocks[pl.ds(kept, 64), :].astype(bf16)
        give_ref[q * 64 : (q + 1) * 64, :] = blocks[pl.ds(given, 64), :].astype(bf16)


def input_kernel(pg_ref, k_ref, out_ref, ps):
    shift_columns(pg_ref[...].astype(f32), ps)
    for g in range(GROUPS):
        cols = slice(g * CG, (g + 1) * CG)
        patches = jnp.concatenate([window(ps, cols, 2 - t // 3, 2 - t % 3) for t in range(9)], 1)
        taps = jnp.concatenate([k_ref[cols, t * CG : (t + 1) * CG] for t in range(9)], 0)
        back = jnp.dot(patches, taps, preferred_element_type=f32).astype(bf16)
        for n in range(2):
            for h in range(SIDE):
                at = n * OUT + h * 16
                out_ref[n, h, :, cols] = back[at : at + SIDE]


def reduce_kernel(part_ref, mean_ref, square_ref, master_ref, out_ref):
    total = part_ref[0:ROWS, :].astype(f32)
    for i in range(1, 64):
        total = total + part_ref[i * ROWS : (i + 1) * ROWS, :].astype(f32)
    for i in range(4):
        out_ref[i, 0:32, :] = total
        out_ref[i, 32:40, :] = mean_ref[...]
        out_ref[i, 40:48, :] = square_ref[...]
        out_ref[i, 48:56, :] = master_ref[...]


def adam(moment_mean, moment_square, master, grad):
    mean_next = 0.9 * moment_mean + 0.1 * grad
    square_next = 0.999 * moment_square + 0.001 * grad * grad
    fix_mean = 1.0 - 0.9**ADAM_STEP
    fix_square = 1.0 - 0.999**ADAM_STEP
    update = mean_next / fix_mean / (jnp.sqrt(square_next / fix_square) + 1e-08)
    return mean_next, square_next, master - 0.02 * update


def adam_kernel(in_ref, gain_ref, grad_ref, send_ref, frame):
    lane = lax.broadcasted_iota(jnp.int32, (8, CG), 1)
    frame[...] = jnp.zeros_like(frame)
    for p in range(4):
        base, shift = divmod(p * SHARD, CG)
        for k in range(3):
            rows = in_ref[p, 32 + 8 * k : 40 + 8 * k, :]
            if shift:
                rows = pltpu.roll(rows, shift, 1)
            frame[k, base : base + 8, :] += jnp.where(lane >= shift, rows, 0.0)
            if shift:
                frame[k, base + 1 : base + 9, :] += jnp.where(lane < shift, rows, 0.0)
    grad = (in_ref[0, 0:32, :] + in_ref[1, 0:32, :]) + (in_ref[2, 0:32, :] + in_ref[3, 0:32, :])
    grad_ref[...] = grad
    master = adam(frame[0, 0:32, :], frame[1, 0:32, :], frame[2, 0:32, :], grad)[2]
    row = lax.broadcasted_iota(jnp.int32, (32, CG), 0)
    block = (lax.axis_index("z") * 4 + lax.axis_index("yh")) * 4 + lax.axis_index("co") * 2 + lax.axis_index("yl")
    mean_of = jnp.zeros((32, CG), f32)
    scale_of = jnp.zeros((32, CG), f32)
    for r in range(3):
        mine = (row >= 9 * r) & (row < 9 * r + 9)
        values = jnp.where(mine, master, 0.0)
        mean = jnp.sum(jnp.sum(values, 0, keepdims=True), 1, keepdims=True) / FAN
        square = jnp.sum(jnp.sum(values * values, 0, keepdims=True), 1, keepdims=True) / FAN
        scale = gain_ref[block * 3 + r] / jnp.sqrt(FAN * (square - mean * mean) + 0.0001)
        mean_of = jnp.where(mine, mean, mean_of)
        scale_of = jnp.where(mine, scale, scale_of)
    out = ((master - mean_of) * scale_of).astype(bf16)
    for i in range(64):
        send_ref[i * ROWS : (i + 1) * ROWS, :] = out


def assemble_kernel(own_ref, got_ref, out_ref, blocks, taps):
    me = lax.axis_index("co")
    for q in range(32):
        kept = pl.multiple_of((2 * q + me) * 64, 64)
        given = pl.multiple_of((2 * q + 1 - me) * 64, 64)
        blocks[pl.ds(kept, 64), :] = own_ref[q * 64 : (q + 1) * 64, :].astype(f32)
        blocks[pl.ds(given, 64), :] = got_ref[q * 64 : (q + 1) * 64, :].astype(f32)
    for t in range(9):
        for r in range(3):
            taps[t, pl.ds(r, BLOCKS, 3), :] = blocks[pl.ds(9 * r + t, BLOCKS, ROWS), :]
    for t in range(9):
        out_ref[:, t * CG : (t + 1) * CG] = taps[t].astype(bf16)


def shape(dims, dtype):
    return jax.ShapeDtypeStruct(dims, dtype)


def swap_cores(x):
    return lax.ppermute(x, "co", [(0, 1), (1, 0)])


def exchange(x, axes):
    return lax.all_to_all(x, axes, 0, 0, tiled=True)


def on_device(
    activations, cotangent, kernel, channel_gain, master_flat, moment_mean, moment_square
):
    pre_grad, keep, give = pl.pallas_call(
        grads_kernel,
        out_shape=(
            shape((2 * IMG, CMID), bf16),
            shape((64 * ROWS, CG), bf16),
            shape((64 * ROWS, CG), bf16),
        ),
        in_specs=[VMEM] * 3,
        out_specs=(VMEM,) * 3,
        scratch_shapes=[
            pltpu.VMEM((2 * IMG, CMID), f32),
            pltpu.VMEM((3, 2 * IMG, CMID), bf16),
            pltpu.VMEM((2 * OUT, CMID), f32),
            pltpu.VMEM((9, CMID, CG), f32),
            pltpu.VMEM((BLOCKS * ROWS, CG), f32),
        ],
        compiler_params=grant(20),
        name="grads",
    )(activations, cotangent, kernel)
    got = swap_cores(give)
    input_grad = pl.pallas_call(
        input_kernel,
        out_shape=shape((2, SIDE, SIDE, CMID), bf16),
        in_specs=[VMEM] * 2,
        out_specs=VMEM,
        scratch_shapes=[pltpu.VMEM((3, 2 * IMG, CMID), bf16)],
        compiler_params=grant(12),
        name="input_grad",
    )(pre_grad, kernel)
    pair = (keep.astype(f32) + got.astype(f32)).astype(bf16)
    parts = exchange(pair.reshape(64, ROWS, CG), ZY)
    parts, input_grad = lax.optimization_barrier((parts, input_grad))
    padded = [
        jnp.pad(flat, (0, 1024 - SHARD)).reshape(8, CG)
        for flat in (moment_mean, moment_square, master_flat)
    ]
    payload = pl.pallas_call(
        reduce_kernel,
        out_shape=shape((4, 56, CG), f32),
        in_specs=[VMEM] * 4,
        out_specs=VMEM,
        compiler_params=grant(4),
        name="reduce",
    )(parts.reshape(64 * ROWS, CG), *padded)
    gathered = exchange(payload, "x")
    grad, send = pl.pallas_call(
        adam_kernel,
        out_shape=(shape((ROWS, CG), f32), shape((64 * ROWS, CG), bf16)),
        in_specs=[VMEM, SMEM],
        out_specs=(VMEM,) * 2,
        scratch_shapes=[pltpu.VMEM((3, 40, CG), f32)],
        compiler_params=grant(4),
        name="adam",
    )(gathered, channel_gain)
    own = exchange(send.reshape(64, ROWS, CG), ZY).reshape(64 * ROWS, CG)
    other = swap_cores(own)
    grad_shard = lax.dynamic_slice(
        grad.reshape(ROWS * CG), (lax.axis_index("x") * SHARD,), (SHARD,)
    )
    mean_next, square_next, master_next = adam(
        moment_mean, moment_square, master_flat, grad_shard
    )
    kernel_next = pl.pallas_call(
        assemble_kernel,
        out_shape=shape((CMID, FAN), bf16),
        in_specs=[VMEM] * 2,
        out_specs=VMEM,
        scratch_shapes=[
            pltpu.VMEM((BLOCKS * ROWS, CG), f32),
            pltpu.VMEM((9, CMID, CG), f32),
        ],
        compiler_params=grant(10),
        name="assemble",
    )(own, other)
    return (input_grad, master_next, mean_next, square_next, kernel_next)


def solution(mesh):
    fine = Mesh(mesh.devices.reshape(SIZES), AXES)
    images = P(AXES, None, None, None)
    state = P(AXES)
    return jax.shard_map(
        on_device,
        mesh=fine,
        in_specs=(images, images, P(), P(), state, state, state),
        out_specs=(images, state, state, state, P()),
        check_vma=False,
    )
```

```python
import jax
import jax.numpy as jnp
from jax import lax
from jax.experimental import pallas as pl
from jax.experimental.pallas import tpu as pltpu
from jax.sharding import Mesh, PartitionSpec as P

CMID = 384
CG = 128
ADAM_STEP = 10
GROUPS = 3
FAN = 1152
SIDE = 14
SHARD = 864
HALF_ROOT = 0.7071067811865476
INV_ROOT_TAU = 0.3989422804014327
bf16 = jnp.bfloat16
f32 = jnp.float32

AXES = ("z", "yh", "co", "yl", "x")
SIZES = (8, 4, 2, 2, 4)
ZY = ("z", "yh", "yl")
BLOCKS = CMID // 3
USED = 27
ROWS = 32
IMG = 256
OUT = SIDE * 16
VMEM = pl.BlockSpec(memory_space=pltpu.VMEM)
SMEM = pl.BlockSpec(memory_space=pltpu.SMEM)


def grant(mib):
    return pltpu.CompilerParams(vmem_limit_bytes=mib * 2**20)


def gelu_slope(values):
    return (
        0.5 * (1.0 + lax.erf(values * HALF_ROOT))
        + values * jnp.exp(-0.5 * values * values) * INV_ROOT_TAU
    )


def shift_columns(full, shifted):
    shifted[0] = pltpu.roll(full, 1, 0).astype(bf16)
    shifted[1] = full.astype(bf16)
    shifted[2] = pltpu.roll(full, full.shape[0] - 1, 0).astype(bf16)


def window(shifted, cols, row_off, col_off):
    return jnp.concatenate(
        [shifted[col_off, n * IMG + row_off * 16 : n * IMG + row_off * 16 + OUT, cols] for n in range(2)],
        0,
    )


def grads_kernel(x_ref, cot_ref, k_ref, pg_ref, keep_ref, give_ref, xf, xs, cf, taps, blocks):
    me = lax.axis_index("co")
    xf[...] = jnp.zeros_like(xf)
    cf[...] = jnp.zeros_like(cf)
    for n in range(2):
        for h in range(SIDE):
            at = n * IMG + (h + 1) * 16
            xf[at : at + SIDE, :] = x_ref[n, h].astype(f32)
            at = n * OUT + h * 16
            cf[at : at + SIDE, :] = cot_ref[n, h].astype(f32)
    shift_columns(xf[...], xs)
    pg_ref[...] = jnp.zeros_like(pg_ref)
    for g in range(GROUPS):
        cols = slice(g * CG, (g + 1) * CG)
        patches = jnp.concatenate([window(xs, cols, t // 3, t % 3) for t in range(9)], 1)
        pre = lax.dot_general(
            patches, k_ref[cols, :], (((1,), (1,)), ((), ())), preferred_element_type=f32
        )
        pg = (cf[:, cols] * gelu_slope(pre)).astype(bf16)
        for n in range(2):
            pg_ref[n * IMG + 16 : n * IMG + 16 + OUT, cols] = pg[n * OUT : (n + 1) * OUT]
        grad = lax.dot_general(pg, patches, (((0,), (0,)), ((), ())), preferred_element_type=f32)
        for t in range(9):
            taps[t, cols, :] = grad[:, t * CG : (t + 1) * CG]
    for t in range(9):
        for r in range(3):
            blocks[pl.ds(9 * r + t, BLOCKS, ROWS), :] = taps[t, pl.ds(r, BLOCKS, 3), :]
    for s in range(USED, ROWS):
        blocks[pl.ds(s, BLOCKS, ROWS), :] = jnp.zeros((BLOCKS, CG), f32)
    for q in range(32):
        kept = pl.multiple_of((2 * q + me) * 64, 64)
        given = pl.multiple_of((2 * q + 1 - me) * 64, 64)
        keep_ref[q * 64 : (q + 1) * 64, :] = blocks[pl.ds(kept, 64), :].astype(bf16)
        give_ref[q * 64 : (q + 1) * 64, :] = blocks[pl.ds(given, 64), :].astype(bf16)


def input_kernel(pg_ref, k_ref, out_ref, ps):
    shift_columns(pg_ref[...].astype(f32), ps)
    for g in range(GROUPS):
        cols = slice(g * CG, (g + 1) * CG)
        patches = jnp.concatenate([window(ps, cols, 2 - t // 3, 2 - t % 3) for t in range(9)], 1)
        taps = jnp.concatenate([k_ref[cols, t * CG : (t + 1) * CG] for t in range(9)], 0)
        back = jnp.dot(patches, taps, preferred_element_type=f32).astype(bf16)
        for n in range(2):
            for h in range(SIDE):
                at = n * OUT + h * 16
                out_ref[n, h, :, cols] = back[at : at + SIDE]


def reduce_kernel(part_ref, mean_ref, square_ref, master_ref, out_ref):
    total = part_ref[0:ROWS, :].astype(f32)
    for i in range(1, 64):
        total = total + part_ref[i * ROWS : (i + 1) * ROWS, :].astype(f32)
    for i in range(4):
        out_ref[i, 0:32, :] = total
        out_ref[i, 32:56, :] = jnp.zeros((24, CG), f32)
    for k, ref in enumerate((mean_ref, square_ref, master_ref)):
        for row in range(7):
            at = 32 + 8 * k + row
            some = min(CG, SHARD - row * CG)
            values = ref[pl.ds(row * CG, some)].reshape(1, some)
            for i in range(4):
                out_ref[i, at : at + 1, 0:some] = values


def adam(moment_mean, moment_square, master, grad):
    mean_next = 0.9 * moment_mean + 0.1 * grad
    square_next = 0.999 * moment_square + 0.001 * grad * grad
    fix_mean = 1.0 - 0.9**ADAM_STEP
    fix_square = 1.0 - 0.999**ADAM_STEP
    update = mean_next / fix_mean / (jnp.sqrt(square_next / fix_square) + 1e-08)
    return mean_next, square_next, master - 0.02 * update


def adam_kernel(in_ref, gain_ref, grad_ref, send_ref, frame):
    lane = lax.broadcasted_iota(jnp.int32, (8, CG), 1)
    frame[...] = jnp.zeros_like(frame)
    for p in range(4):
        base, shift = divmod(p * SHARD, CG)
        for k in range(3):
            rows = in_ref[p, 32 + 8 * k : 40 + 8 * k, :]
            if shift:
                rows = pltpu.roll(rows, shift, 1)
            frame[k, base : base + 8, :] += jnp.where(lane >= shift, rows, 0.0)
            if shift:
                frame[k, base + 1 : base + 9, :] += jnp.where(lane < shift, rows, 0.0)
    grad = (in_ref[0, 0:32, :] + in_ref[1, 0:32, :]) + (in_ref[2, 0:32, :] + in_ref[3, 0:32, :])
    grad_ref[...] = grad
    master = adam(frame[0, 0:32, :], frame[1, 0:32, :], frame[2, 0:32, :], grad)[2]
    row = lax.broadcasted_iota(jnp.int32, (32, CG), 0)
    block = (lax.axis_index("z") * 4 + lax.axis_index("yh")) * 4 + lax.axis_index("co") * 2 + lax.axis_index("yl")
    mean_of = jnp.zeros((32, CG), f32)
    scale_of = jnp.zeros((32, CG), f32)
    for r in range(3):
        mine = (row >= 9 * r) & (row < 9 * r + 9)
        values = jnp.where(mine, master, 0.0)
        mean = jnp.sum(jnp.sum(values, 0, keepdims=True), 1, keepdims=True) / FAN
        square = jnp.sum(jnp.sum(values * values, 0, keepdims=True), 1, keepdims=True) / FAN
        scale = gain_ref[block * 3 + r] / jnp.sqrt(FAN * (square - mean * mean) + 0.0001)
        mean_of = jnp.where(mine, mean, mean_of)
        scale_of = jnp.where(mine, scale, scale_of)
    out = ((master - mean_of) * scale_of).astype(bf16)
    for i in range(64):
        send_ref[i * ROWS : (i + 1) * ROWS, :] = out


def assemble_kernel(own_ref, got_ref, out_ref, blocks, taps):
    me = lax.axis_index("co")
    for q in range(32):
        kept = pl.multiple_of((2 * q + me) * 64, 64)
        given = pl.multiple_of((2 * q + 1 - me) * 64, 64)
        blocks[pl.ds(kept, 64), :] = own_ref[q * 64 : (q + 1) * 64, :].astype(f32)
        blocks[pl.ds(given, 64), :] = got_ref[q * 64 : (q + 1) * 64, :].astype(f32)
    for t in range(9):
        for r in range(3):
            taps[t, pl.ds(r, BLOCKS, 3), :] = blocks[pl.ds(9 * r + t, BLOCKS, ROWS), :]
    for t in range(9):
        out_ref[:, t * CG : (t + 1) * CG] = taps[t].astype(bf16)


def shape(dims, dtype):
    return jax.ShapeDtypeStruct(dims, dtype)


def swap_cores(x):
    return lax.ppermute(x, "co", [(0, 1), (1, 0)])


def exchange(x, axes):
    return lax.all_to_all(x, axes, 0, 0, tiled=True)


def on_device(
    activations, cotangent, kernel, channel_gain, master_flat, moment_mean, moment_square
):
    pre_grad, keep, give = pl.pallas_call(
        grads_kernel,
        out_shape=(
            shape((2 * IMG, CMID), bf16),
            shape((64 * ROWS, CG), bf16),
            shape((64 * ROWS, CG), bf16),
        ),
        in_specs=[VMEM] * 3,
        out_specs=(VMEM,) * 3,
        scratch_shapes=[
            pltpu.VMEM((2 * IMG, CMID), f32),
            pltpu.VMEM((3, 2 * IMG, CMID), bf16),
            pltpu.VMEM((2 * OUT, CMID), f32),
            pltpu.VMEM((9, CMID, CG), f32),
            pltpu.VMEM((BLOCKS * ROWS, CG), f32),
        ],
        compiler_params=grant(20),
        name="grads",
    )(activations, cotangent, kernel)
    got = swap_cores(give)
    input_grad = pl.pallas_call(
        input_kernel,
        out_shape=shape((2, SIDE, SIDE, CMID), bf16),
        in_specs=[VMEM] * 2,
        out_specs=VMEM,
        scratch_shapes=[pltpu.VMEM((3, 2 * IMG, CMID), bf16)],
        compiler_params=grant(12),
        name="input_grad",
    )(pre_grad, kernel)
    pair = (keep.astype(f32) + got.astype(f32)).astype(bf16)
    pair, input_grad = lax.optimization_barrier((pair, input_grad))
    parts = exchange(pair.reshape(64, ROWS, CG), ZY)
    payload = pl.pallas_call(
        reduce_kernel,
        out_shape=shape((4, 56, CG), f32),
        in_specs=[VMEM] * 4,
        out_specs=VMEM,
        compiler_params=grant(4),
        name="reduce",
    )(parts.reshape(64 * ROWS, CG), moment_mean, moment_square, master_flat)
    gathered = exchange(payload, "x")
    grad, send = pl.pallas_call(
        adam_kernel,
        out_shape=(shape((ROWS, CG), f32), shape((64 * ROWS, CG), bf16)),
        in_specs=[VMEM, SMEM],
        out_specs=(VMEM,) * 2,
        scratch_shapes=[pltpu.VMEM((3, 40, CG), f32)],
        compiler_params=grant(4),
        name="adam",
    )(gathered, channel_gain)
    own = exchange(send.reshape(64, ROWS, CG), ZY).reshape(64 * ROWS, CG)
    other = swap_cores(own)
    grad_shard = lax.dynamic_slice(
        grad.reshape(ROWS * CG), (lax.axis_index("x") * SHARD,), (SHARD,)
    )
    mean_next, square_next, master_next = adam(
        moment_mean, moment_square, master_flat, grad_shard
    )
    kernel_next = pl.pallas_call(
        assemble_kernel,
        out_shape=shape((CMID, FAN), bf16),
        in_specs=[VMEM] * 2,
        out_specs=VMEM,
        scratch_shapes=[
            pltpu.VMEM((BLOCKS * ROWS, CG), f32),
            pltpu.VMEM((9, CMID, CG), f32),
        ],
        compiler_params=grant(10),
        name="assemble",
    )(own, other)
    return (input_grad, master_next, mean_next, square_next, kernel_next)


def solution(mesh):
    fine = Mesh(mesh.devices.reshape(SIZES), AXES)
    images = P(AXES, None, None, None)
    state = P(AXES)
    return jax.shard_map(
        on_device,
        mesh=fine,
        in_specs=(images, images, P(), P(), state, state, state),
        out_specs=(images, state, state, state, P()),
        check_vma=False,
    )
```

```python
import jax
import jax.numpy as jnp
from jax import lax
from jax.experimental import pallas as pl
from jax.experimental.pallas import tpu as pltpu
from jax.sharding import Mesh, PartitionSpec as P

CMID = 384
CG = 128
ADAM_STEP = 10
GROUPS = 3
FAN = 1152
SIDE = 14
SHARD = 864
HALF_ROOT = 0.7071067811865476
INV_ROOT_TAU = 0.3989422804014327
bf16 = jnp.bfloat16
f32 = jnp.float32

AXES = ("z", "yh", "co", "yl", "x")
SIZES = (8, 4, 2, 2, 4)
ZY = ("z", "yh", "yl")
BLOCKS = CMID // 3
USED = 27
ROWS = 32
IMG = 256
OUT = SIDE * 16
VMEM = pl.BlockSpec(memory_space=pltpu.VMEM)
SMEM = pl.BlockSpec(memory_space=pltpu.SMEM)


def grant(mib):
    return pltpu.CompilerParams(vmem_limit_bytes=mib * 2**20)


def gelu_slope(values):
    return (
        0.5 * (1.0 + lax.erf(values * HALF_ROOT))
        + values * jnp.exp(-0.5 * values * values) * INV_ROOT_TAU
    )


def shift_columns(full, shifted):
    shifted[0] = pltpu.roll(full, 1, 0).astype(bf16)
    shifted[1] = full.astype(bf16)
    shifted[2] = pltpu.roll(full, full.shape[0] - 1, 0).astype(bf16)


def window(shifted, cols, row_off, col_off):
    return jnp.concatenate(
        [shifted[col_off, n * IMG + row_off * 16 : n * IMG + row_off * 16 + OUT, cols] for n in range(2)],
        0,
    )


def widen(cells):
    return jnp.concatenate([cells.astype(f32), jnp.zeros((2, CMID), f32)], 0)


def grads_kernel(x_ref, cot_ref, k_ref, pg_ref, keep_ref, give_ref, xf, xs, cf, taps, blocks):
    me = lax.axis_index("co")
    for n in range(2):
        for at in (n * IMG, n * IMG + 240):
            xf[at : at + 16, :] = jnp.zeros((16, CMID), f32)
            pg_ref[at : at + 16, :] = jnp.zeros((16, CMID), bf16)
        for h in range(SIDE):
            at = n * IMG + (h + 1) * 16
            xf[at : at + 16, :] = widen(x_ref[n, h])
            at = n * OUT + h * 16
            cf[at : at + 16, :] = widen(cot_ref[n, h])
    shift_columns(xf[...], xs)
    def group(g):
        cols = slice(g * CG, (g + 1) * CG)
        return cols, jnp.concatenate([window(xs, cols, t // 3, t % 3) for t in range(9)], 1)

    def forward(g):
        cols, patches = group(g)
        return lax.dot_general(
            patches, k_ref[cols, :], (((1,), (1,)), ((), ())), preferred_element_type=f32
        )

    def slope(g, pre):
        cols = slice(g * CG, (g + 1) * CG)
        pg = (cf[:, cols] * gelu_slope(pre)).astype(bf16)
        for n in range(2):
            pg_ref[n * IMG + 16 : n * IMG + 16 + OUT, cols] = pg[n * OUT : (n + 1) * OUT]
        return pg

    def weight(g, pg):
        cols, patches = group(g)
        grad = lax.dot_general(pg, patches, (((0,), (0,)), ((), ())), preferred_element_type=f32)
        for t in range(9):
            taps[t, cols, :] = grad[:, t * CG : (t + 1) * CG]

    pre = [forward(g) for g in range(GROUPS)]
    for g in range(GROUPS):
        weight(g, slope(g, pre[g]))
    for t in range(9):
        for r in range(3):
            blocks[pl.ds(9 * r + t, BLOCKS, USED), :] = taps[t, pl.ds(r, BLOCKS, 3), :]
    blocks[BLOCKS * USED :, :] = jnp.zeros((8, CG), f32)
    for core in range(2):

        @pl.when(me == core)
        def _():
            for q in range(64):
                kept = (q // 2 * 4 + 2 * core + q % 2) * USED
                given = (q // 2 * 4 + 2 - 2 * core + q % 2) * USED
                keep_ref[q * ROWS : (q + 1) * ROWS, :] = blocks[kept : kept + ROWS, :].astype(bf16)
                give_ref[q * ROWS : (q + 1) * ROWS, :] = blocks[given : given + ROWS, :].astype(bf16)


def input_kernel(pg_ref, k_ref, out_ref, ps):
    shift_columns(pg_ref[...].astype(f32), ps)
    for g in range(GROUPS):
        cols = slice(g * CG, (g + 1) * CG)
        patches = jnp.concatenate([window(ps, cols, 2 - t // 3, 2 - t % 3) for t in range(9)], 1)
        taps = jnp.concatenate([k_ref[cols, t * CG : (t + 1) * CG] for t in range(9)], 0)
        back = jnp.dot(patches, taps, preferred_element_type=f32).astype(bf16)
        for n in range(2):
            for h in range(SIDE):
                at = n * OUT + h * 16
                out_ref[n, h, :, cols] = back[at : at + SIDE]


def reduce_kernel(part_ref, mean_ref, square_ref, master_ref, out_ref):
    total = part_ref[0:ROWS, :].astype(f32)
    for i in range(1, 64):
        total = total + part_ref[i * ROWS : (i + 1) * ROWS, :].astype(f32)
    for i in range(4):
        out_ref[i, 0:32, :] = total
        out_ref[i, 32:56, :] = jnp.zeros((24, CG), f32)
    for k, ref in enumerate((mean_ref, square_ref, master_ref)):
        for row in range(7):
            at = 32 + 8 * k + row
            some = min(CG, SHARD - row * CG)
            values = ref[pl.ds(row * CG, some)].reshape(1, some)
            for i in range(4):
                out_ref[i, at : at + 1, 0:some] = values


def adam(moment_mean, moment_square, master, grad):
    mean_next = 0.9 * moment_mean + 0.1 * grad
    square_next = 0.999 * moment_square + 0.001 * grad * grad
    fix_mean = 1.0 - 0.9**ADAM_STEP
    fix_square = 1.0 - 0.999**ADAM_STEP
    update = mean_next / fix_mean / (jnp.sqrt(square_next / fix_square) + 1e-08)
    return mean_next, square_next, master - 0.02 * update


def adam_kernel(in_ref, gain_ref, grad_ref, send_ref, frame):
    lane = lax.broadcasted_iota(jnp.int32, (8, CG), 1)
    frame[...] = jnp.zeros_like(frame)
    for p in range(4):
        base, shift = divmod(p * SHARD, CG)
        for k in range(3):
            rows = in_ref[p, 32 + 8 * k : 40 + 8 * k, :]
            if shift:
                rows = pltpu.roll(rows, shift, 1)
            frame[k, base : base + 8, :] += jnp.where(lane >= shift, rows, 0.0)
            if shift:
                frame[k, base + 1 : base + 9, :] += jnp.where(lane < shift, rows, 0.0)
    grad = (in_ref[0, 0:32, :] + in_ref[1, 0:32, :]) + (in_ref[2, 0:32, :] + in_ref[3, 0:32, :])
    grad_ref[...] = grad
    master = adam(frame[0, 0:32, :], frame[1, 0:32, :], frame[2, 0:32, :], grad)[2]
    row = lax.broadcasted_iota(jnp.int32, (32, CG), 0)
    block = (lax.axis_index("z") * 4 + lax.axis_index("yh")) * 4 + lax.axis_index("co") * 2 + lax.axis_index("yl")
    mean_of = jnp.zeros((32, CG), f32)
    scale_of = jnp.zeros((32, CG), f32)
    for r in range(3):
        mine = (row >= 9 * r) & (row < 9 * r + 9)
        values = jnp.where(mine, master, 0.0)
        mean = jnp.sum(jnp.sum(values, 0, keepdims=True), 1, keepdims=True) / FAN
        square = jnp.sum(jnp.sum(values * values, 0, keepdims=True), 1, keepdims=True) / FAN
        scale = gain_ref[block * 3 + r] / jnp.sqrt(FAN * (square - mean * mean) + 0.0001)
        mean_of = jnp.where(mine, mean, mean_of)
        scale_of = jnp.where(mine, scale, scale_of)
    out = ((master - mean_of) * scale_of).astype(bf16)
    for i in range(64):
        send_ref[i * ROWS : (i + 1) * ROWS, :] = out


def assemble_kernel(own_ref, got_ref, out_ref, blocks, taps):
    me = lax.axis_index("co")
    for core in range(2):

        @pl.when(me == core)
        def _():
            for q in range(64):
                kept = (q // 2 * 4 + 2 * core + q % 2) * USED
                given = (q // 2 * 4 + 2 - 2 * core + q % 2) * USED
                blocks[kept : kept + USED, :] = own_ref[q * ROWS : q * ROWS + USED, :].astype(f32)
                blocks[given : given + USED, :] = got_ref[q * ROWS : q * ROWS + USED, :].astype(f32)

    for t in range(9):
        for r in range(3):
            taps[t, pl.ds(r, BLOCKS, 3), :] = blocks[pl.ds(9 * r + t, BLOCKS, USED), :]
    for t in range(9):
        out_ref[:, t * CG : (t + 1) * CG] = taps[t].astype(bf16)


def shape(dims, dtype):
    return jax.ShapeDtypeStruct(dims, dtype)


def swap_cores(x):
    return lax.ppermute(x, "co", [(0, 1), (1, 0)])


def exchange(x, axes):
    return lax.all_to_all(x, axes, 0, 0, tiled=True)


def on_device(
    activations, cotangent, kernel, channel_gain, master_flat, moment_mean, moment_square
):
    pre_grad, keep, give = pl.pallas_call(
        grads_kernel,
        out_shape=(
            shape((2 * IMG, CMID), bf16),
            shape((64 * ROWS, CG), bf16),
            shape((64 * ROWS, CG), bf16),
        ),
        in_specs=[VMEM] * 3,
        out_specs=(VMEM,) * 3,
        scratch_shapes=[
            pltpu.VMEM((2 * IMG, CMID), f32),
            pltpu.VMEM((3, 2 * IMG, CMID), bf16),
            pltpu.VMEM((2 * OUT, CMID), f32),
            pltpu.VMEM((9, CMID, CG), f32),
            pltpu.VMEM((BLOCKS * USED + 8, CG), f32),
        ],
        compiler_params=grant(20),
        name="grads",
    )(activations, cotangent, kernel)
    got = swap_cores(give)
    input_grad = pl.pallas_call(
        input_kernel,
        out_shape=shape((2, SIDE, SIDE, CMID), bf16),
        in_specs=[VMEM] * 2,
        out_specs=VMEM,
        scratch_shapes=[pltpu.VMEM((3, 2 * IMG, CMID), bf16)],
        compiler_params=grant(12),
        name="input_grad",
    )(pre_grad, kernel)
    pair = (keep.astype(f32) + got.astype(f32)).astype(bf16)
    pair, input_grad = lax.optimization_barrier((pair, input_grad))
    parts = exchange(pair.reshape(64, ROWS, CG), ZY)
    payload = pl.pallas_call(
        reduce_kernel,
        out_shape=shape((4, 56, CG), f32),
        in_specs=[VMEM] * 4,
        out_specs=VMEM,
        compiler_params=grant(4),
        name="reduce",
    )(parts.reshape(64 * ROWS, CG), moment_mean, moment_square, master_flat)
    gathered = exchange(payload, "x")
    grad, send = pl.pallas_call(
        adam_kernel,
        out_shape=(shape((ROWS, CG), f32), shape((64 * ROWS, CG), bf16)),
        in_specs=[VMEM, SMEM],
        out_specs=(VMEM,) * 2,
        scratch_shapes=[pltpu.VMEM((3, 40, CG), f32)],
        compiler_params=grant(4),
        name="adam",
    )(gathered, channel_gain)
    own = exchange(send.reshape(64, ROWS, CG), ZY).reshape(64 * ROWS, CG)
    other = swap_cores(own)
    grad_shard = lax.dynamic_slice(
        grad.reshape(ROWS * CG), (lax.axis_index("x") * SHARD,), (SHARD,)
    )
    mean_next, square_next, master_next = adam(
        moment_mean, moment_square, master_flat, grad_shard
    )
    kernel_next = pl.pallas_call(
        assemble_kernel,
        out_shape=shape((CMID, FAN), bf16),
        in_specs=[VMEM] * 2,
        out_specs=VMEM,
        scratch_shapes=[
            pltpu.VMEM((BLOCKS * USED + 8, CG), f32),
            pltpu.VMEM((9, CMID, CG), f32),
        ],
        compiler_params=grant(10),
        name="assemble",
    )(own, other)
    return (input_grad, master_next, mean_next, square_next, kernel_next)


def solution(mesh):
    fine = Mesh(mesh.devices.reshape(SIZES), AXES)
    images = P(AXES, None, None, None)
    state = P(AXES)
    return jax.shard_map(
        on_device,
        mesh=fine,
        in_specs=(images, images, P(), P(), state, state, state),
        out_specs=(images, state, state, state, P()),
        check_vma=False,
    )
```

```python
import jax
import jax.numpy as jnp
from jax import lax
from jax.experimental import pallas as pl
from jax.experimental.pallas import tpu as pltpu
from jax.sharding import Mesh, PartitionSpec as P

CMID = 384
CG = 128
ADAM_STEP = 10
GROUPS = 3
FAN = 1152
SIDE = 14
SHARD = 864
HALF_ROOT = 0.7071067811865476
INV_ROOT_TAU = 0.3989422804014327
bf16 = jnp.bfloat16
f32 = jnp.float32

AXES = ("z", "yh", "co", "yl", "x")
SIZES = (8, 4, 2, 2, 4)
ZY = ("z", "yh", "yl")
BLOCKS = CMID // 3
USED = 27
ROWS = 32
TILES = 7
IMG = 256
OUT = SIDE * 16
VMEM = pl.BlockSpec(memory_space=pltpu.VMEM)
SMEM = pl.BlockSpec(memory_space=pltpu.SMEM)


def grant(mib):
    return pltpu.CompilerParams(vmem_limit_bytes=mib * 2**20)


def gelu_slope(values):
    return (
        0.5 * (1.0 + lax.erf(values * HALF_ROOT))
        + values * jnp.exp(-0.5 * values * values) * INV_ROOT_TAU
    )


def shift_columns(full, shifted):
    shifted[0] = pltpu.roll(full, 1, 0).astype(bf16)
    shifted[1] = full.astype(bf16)
    shifted[2] = pltpu.roll(full, full.shape[0] - 1, 0).astype(bf16)


def window(shifted, cols, row_off, col_off):
    return jnp.concatenate(
        [shifted[col_off, n * IMG + row_off * 16 : n * IMG + row_off * 16 + OUT, cols] for n in range(2)],
        0,
    )


def widen(cells):
    return jnp.concatenate([cells.astype(f32), jnp.zeros((2, CMID), f32)], 0)


def grads_kernel(x_ref, cot_ref, k_ref, pg_ref, keep_ref, give_ref, xf, xs, cf, taps, blocks):
    me = lax.axis_index("co")
    for n in range(2):
        for at in (n * IMG, n * IMG + 240):
            xf[at : at + 16, :] = jnp.zeros((16, CMID), f32)
            pg_ref[at : at + 16, :] = jnp.zeros((16, CMID), bf16)
        for h in range(SIDE):
            at = n * IMG + (h + 1) * 16
            xf[at : at + 16, :] = widen(x_ref[n, h])
            at = n * OUT + h * 16
            cf[at : at + 16, :] = widen(cot_ref[n, h])
    shift_columns(xf[...], xs)
    def group(g):
        cols = slice(g * CG, (g + 1) * CG)
        return cols, jnp.concatenate([window(xs, cols, t // 3, t % 3) for t in range(9)], 1)

    def forward(g):
        cols, patches = group(g)
        return lax.dot_general(
            patches, k_ref[cols, :], (((1,), (1,)), ((), ())), preferred_element_type=f32
        )

    def slope(g, pre):
        cols = slice(g * CG, (g + 1) * CG)
        pg = (cf[:, cols] * gelu_slope(pre)).astype(bf16)
        for n in range(2):
            pg_ref[n * IMG + 16 : n * IMG + 16 + OUT, cols] = pg[n * OUT : (n + 1) * OUT]
        return pg

    def weight(g, pg):
        cols, patches = group(g)
        grad = lax.dot_general(pg, patches, (((0,), (0,)), ((), ())), preferred_element_type=f32)
        for t in range(9):
            taps[t, cols, :] = grad[:, t * CG : (t + 1) * CG]

    pre = [forward(g) for g in range(GROUPS)]
    for g in range(GROUPS):
        weight(g, slope(g, pre[g]))
    for t in range(9):
        for r in range(3):
            blocks[pl.ds(9 * r + t, BLOCKS, USED), :] = taps[t, pl.ds(r, BLOCKS, 3), :]
    blocks[BLOCKS * USED :, :] = jnp.zeros((8, CG), f32)
    for core in range(2):

        @pl.when(me == core)
        def _():
            for q in range(64):
                kept = (q // 2 * 4 + 2 * core + q % 2) * USED
                given = (q // 2 * 4 + 2 - 2 * core + q % 2) * USED
                for k in range(TILES):
                    at = 4 * k
                    keep_ref[q, k] = blocks[kept + at : kept + at + 4, :].astype(bf16)
                    give_ref[q, k] = blocks[given + at : given + at + 4, :].astype(bf16)


def input_kernel(pg_ref, k_ref, out_ref, ps):
    shift_columns(pg_ref[...].astype(f32), ps)
    for g in range(GROUPS):
        cols = slice(g * CG, (g + 1) * CG)
        patches = jnp.concatenate([window(ps, cols, 2 - t // 3, 2 - t % 3) for t in range(9)], 1)
        taps = jnp.concatenate([k_ref[cols, t * CG : (t + 1) * CG] for t in range(9)], 0)
        back = jnp.dot(patches, taps, preferred_element_type=f32).astype(bf16)
        for n in range(2):
            for h in range(SIDE):
                at = n * OUT + h * 16
                out_ref[n, h, :, cols] = back[at : at + SIDE]


def reduce_kernel(part_ref, mean_ref, square_ref, master_ref, out_ref):
    total = part_ref[0].astype(f32)
    for i in range(1, 64):
        total = total + part_ref[i].astype(f32)
    for i in range(4):
        out_ref[i, 24:56, :] = jnp.zeros((32, CG), f32)
        for k in range(TILES):
            out_ref[i, 4 * k : 4 * k + 4, :] = total[k]
    for k, ref in enumerate((mean_ref, square_ref, master_ref)):
        for row in range(7):
            at = 32 + 8 * k + row
            some = min(CG, SHARD - row * CG)
            values = ref[pl.ds(row * CG, some)].reshape(1, some)
            for i in range(4):
                out_ref[i, at : at + 1, 0:some] = values


def adam(moment_mean, moment_square, master, grad):
    mean_next = 0.9 * moment_mean + 0.1 * grad
    square_next = 0.999 * moment_square + 0.001 * grad * grad
    fix_mean = 1.0 - 0.9**ADAM_STEP
    fix_square = 1.0 - 0.999**ADAM_STEP
    update = mean_next / fix_mean / (jnp.sqrt(square_next / fix_square) + 1e-08)
    return mean_next, square_next, master - 0.02 * update


def adam_kernel(in_ref, gain_ref, grad_ref, send_ref, frame):
    lane = lax.broadcasted_iota(jnp.int32, (8, CG), 1)
    frame[...] = jnp.zeros_like(frame)
    for p in range(4):
        base, shift = divmod(p * SHARD, CG)
        for k in range(3):
            rows = in_ref[p, 32 + 8 * k : 40 + 8 * k, :]
            if shift:
                rows = pltpu.roll(rows, shift, 1)
            frame[k, base : base + 8, :] += jnp.where(lane >= shift, rows, 0.0)
            if shift:
                frame[k, base + 1 : base + 9, :] += jnp.where(lane < shift, rows, 0.0)
    grad = (in_ref[0, 0:32, :] + in_ref[1, 0:32, :]) + (in_ref[2, 0:32, :] + in_ref[3, 0:32, :])
    grad_ref[...] = grad
    master = adam(frame[0, 0:32, :], frame[1, 0:32, :], frame[2, 0:32, :], grad)[2]
    row = lax.broadcasted_iota(jnp.int32, (32, CG), 0)
    block = (lax.axis_index("z") * 4 + lax.axis_index("yh")) * 4 + lax.axis_index("co") * 2 + lax.axis_index("yl")
    mean_of = jnp.zeros((32, CG), f32)
    scale_of = jnp.zeros((32, CG), f32)
    for r in range(3):
        mine = (row >= 9 * r) & (row < 9 * r + 9)
        values = jnp.where(mine, master, 0.0)
        mean = jnp.sum(jnp.sum(values, 0, keepdims=True), 1, keepdims=True) / FAN
        square = jnp.sum(jnp.sum(values * values, 0, keepdims=True), 1, keepdims=True) / FAN
        scale = gain_ref[block * 3 + r] / jnp.sqrt(FAN * (square - mean * mean) + 0.0001)
        mean_of = jnp.where(mine, mean, mean_of)
        scale_of = jnp.where(mine, scale, scale_of)
    out = (master - mean_of) * scale_of
    for k in range(TILES):
        tile = out[4 * k : 4 * k + 4].astype(bf16)
        for i in range(64):
            send_ref[i, k] = tile


def assemble_kernel(own_ref, got_ref, out_ref, blocks, taps):
    me = lax.axis_index("co")
    for core in range(2):

        @pl.when(me == core)
        def _():
            for q in range(64):
                kept = (q // 2 * 4 + 2 * core + q % 2) * USED
                given = (q // 2 * 4 + 2 - 2 * core + q % 2) * USED
                for k in range(TILES):
                    at, some = 4 * k, min(4, USED - 4 * k)
                    blocks[kept + at : kept + at + some, :] = own_ref[q, k].astype(f32)[:some]
                    blocks[given + at : given + at + some, :] = got_ref[q, k].astype(f32)[:some]

    for t in range(9):
        for r in range(3):
            taps[t, pl.ds(r, BLOCKS, 3), :] = blocks[pl.ds(9 * r + t, BLOCKS, USED), :]
    for t in range(9):
        out_ref[:, t * CG : (t + 1) * CG] = taps[t].astype(bf16)


def shape(dims, dtype):
    return jax.ShapeDtypeStruct(dims, dtype)


def swap_cores(x):
    return lax.ppermute(x, "co", [(0, 1), (1, 0)])


def exchange(x, axes):
    return lax.all_to_all(x, axes, 0, 0, tiled=True)


def on_device(
    activations, cotangent, kernel, channel_gain, master_flat, moment_mean, moment_square
):
    pre_grad, keep, give = pl.pallas_call(
        grads_kernel,
        out_shape=(
            shape((2 * IMG, CMID), bf16),
            shape((64, TILES, 4, CG), bf16),
            shape((64, TILES, 4, CG), bf16),
        ),
        in_specs=[VMEM] * 3,
        out_specs=(VMEM,) * 3,
        scratch_shapes=[
            pltpu.VMEM((2 * IMG, CMID), f32),
            pltpu.VMEM((3, 2 * IMG, CMID), bf16),
            pltpu.VMEM((2 * OUT, CMID), f32),
            pltpu.VMEM((9, CMID, CG), f32),
            pltpu.VMEM((BLOCKS * USED + 8, CG), f32),
        ],
        compiler_params=grant(20),
        name="grads",
    )(activations, cotangent, kernel)
    got = swap_cores(give)
    input_grad = pl.pallas_call(
        input_kernel,
        out_shape=shape((2, SIDE, SIDE, CMID), bf16),
        in_specs=[VMEM] * 2,
        out_specs=VMEM,
        scratch_shapes=[pltpu.VMEM((3, 2 * IMG, CMID), bf16)],
        compiler_params=grant(12),
        name="input_grad",
    )(pre_grad, kernel)
    pair = (keep.astype(f32) + got.astype(f32)).astype(bf16)
    pair, input_grad = lax.optimization_barrier((pair, input_grad))
    parts = exchange(pair, ZY)
    payload = pl.pallas_call(
        reduce_kernel,
        out_shape=shape((4, 56, CG), f32),
        in_specs=[VMEM] * 4,
        out_specs=VMEM,
        compiler_params=grant(4),
        name="reduce",
    )(parts, moment_mean, moment_square, master_flat)
    gathered = exchange(payload, "x")
    grad, send = pl.pallas_call(
        adam_kernel,
        out_shape=(shape((ROWS, CG), f32), shape((64, TILES, 4, CG), bf16)),
        in_specs=[VMEM, SMEM],
        out_specs=(VMEM,) * 2,
        scratch_shapes=[pltpu.VMEM((3, 40, CG), f32)],
        compiler_params=grant(4),
        name="adam",
    )(gathered, channel_gain)
    own = exchange(send, ZY)
    other = swap_cores(own)
    grad_shard = lax.dynamic_slice(
        grad.reshape(ROWS * CG), (lax.axis_index("x") * SHARD,), (SHARD,)
    )
    mean_next, square_next, master_next = adam(
        moment_mean, moment_square, master_flat, grad_shard
    )
    kernel_next = pl.pallas_call(
        assemble_kernel,
        out_shape=shape((CMID, FAN), bf16),
        in_specs=[VMEM] * 2,
        out_specs=VMEM,
        scratch_shapes=[
            pltpu.VMEM((BLOCKS * USED + 8, CG), f32),
            pltpu.VMEM((9, CMID, CG), f32),
        ],
        compiler_params=grant(10),
        name="assemble",
    )(own, other)
    return (input_grad, master_next, mean_next, square_next, kernel_next)


def solution(mesh):
    fine = Mesh(mesh.devices.reshape(SIZES), AXES)
    images = P(AXES, None, None, None)
    state = P(AXES)
    return jax.shard_map(
        on_device,
        mesh=fine,
        in_specs=(images, images, P(), P(), state, state, state),
        out_specs=(images, state, state, state, P()),
        check_vma=False,
    )
```

```python
import jax
import jax.numpy as jnp
from jax import lax
from jax.experimental import pallas as pl
from jax.experimental.pallas import tpu as pltpu
from jax.sharding import Mesh, PartitionSpec as P

CMID = 384
CG = 128
ADAM_STEP = 10
GROUPS = 3
FAN = 1152
SIDE = 14
SHARD = 864
HALF_ROOT = 0.7071067811865476
INV_ROOT_TAU = 0.3989422804014327
bf16 = jnp.bfloat16
f32 = jnp.float32

AXES = ("z", "yh", "co", "yl", "x")
SIZES = (8, 4, 2, 2, 4)
ZY = ("z", "yh", "yl")
BLOCKS = CMID // 3
USED = 27
ROWS = 32
TILES = 7
IMG = 256
OUT = SIDE * 16
VMEM = pl.BlockSpec(memory_space=pltpu.VMEM)


def grant(mib):
    return pltpu.CompilerParams(vmem_limit_bytes=mib * 2**20)


def gelu_slope(values):
    return (
        0.5 * (1.0 + lax.erf(values * HALF_ROOT))
        + values * jnp.exp(-0.5 * values * values) * INV_ROOT_TAU
    )


def shift_columns(full, shifted):
    shifted[0] = pltpu.roll(full, 1, 0).astype(bf16)
    shifted[1] = full.astype(bf16)
    shifted[2] = pltpu.roll(full, full.shape[0] - 1, 0).astype(bf16)


def window(shifted, cols, row_off, col_off):
    return jnp.concatenate(
        [shifted[col_off, n * IMG + row_off * 16 : n * IMG + row_off * 16 + OUT, cols] for n in range(2)],
        0,
    )


def widen(cells):
    return jnp.concatenate([cells.astype(f32), jnp.zeros((2, CMID), f32)], 0)


def grads_kernel(x_ref, cot_ref, k_ref, pg_ref, keep_ref, give_ref, xf, xs, cf, taps, blocks):
    me = lax.axis_index("co")
    for n in range(2):
        for at in (n * IMG, n * IMG + 240):
            xf[at : at + 16, :] = jnp.zeros((16, CMID), f32)
            pg_ref[at : at + 16, :] = jnp.zeros((16, CMID), bf16)
        for h in range(SIDE):
            at = n * IMG + (h + 1) * 16
            xf[at : at + 16, :] = widen(x_ref[n, h])
            at = n * OUT + h * 16
            cf[at : at + 16, :] = widen(cot_ref[n, h])
    shift_columns(xf[...], xs)
    def group(g):
        cols = slice(g * CG, (g + 1) * CG)
        return cols, jnp.concatenate([window(xs, cols, t // 3, t % 3) for t in range(9)], 1)

    def forward(g):
        cols, patches = group(g)
        return lax.dot_general(
            patches, k_ref[cols, :], (((1,), (1,)), ((), ())), preferred_element_type=f32
        )

    def slope(g, pre):
        cols = slice(g * CG, (g + 1) * CG)
        pg = (cf[:, cols] * gelu_slope(pre)).astype(bf16)
        for n in range(2):
            pg_ref[n * IMG + 16 : n * IMG + 16 + OUT, cols] = pg[n * OUT : (n + 1) * OUT]
        return pg

    def weight(g, pg):
        cols, patches = group(g)
        grad = lax.dot_general(pg, patches, (((0,), (0,)), ((), ())), preferred_element_type=f32)
        for t in range(9):
            taps[t, cols, :] = grad[:, t * CG : (t + 1) * CG]

    pre = [forward(g) for g in range(GROUPS)]
    for g in range(GROUPS):
        weight(g, slope(g, pre[g]))
    for t in range(9):
        for r in range(3):
            blocks[pl.ds(9 * r + t, BLOCKS, USED), :] = taps[t, pl.ds(r, BLOCKS, 3), :]
    blocks[BLOCKS * USED :, :] = jnp.zeros((8, CG), f32)
    for core in range(2):

        @pl.when(me == core)
        def _():
            for q in range(64):
                kept = (q // 2 * 4 + 2 * core + q % 2) * USED
                given = (q // 2 * 4 + 2 - 2 * core + q % 2) * USED
                for k in range(TILES):
                    at = 4 * k
                    keep_ref[q, k] = blocks[kept + at : kept + at + 4, :].astype(bf16)
                    give_ref[q, k] = blocks[given + at : given + at + 4, :].astype(bf16)


def input_kernel(pg_ref, k_ref, out_ref, ps):
    shift_columns(pg_ref[...].astype(f32), ps)
    for g in range(GROUPS):
        cols = slice(g * CG, (g + 1) * CG)
        patches = jnp.concatenate([window(ps, cols, 2 - t // 3, 2 - t % 3) for t in range(9)], 1)
        taps = jnp.concatenate([k_ref[cols, t * CG : (t + 1) * CG] for t in range(9)], 0)
        back = jnp.dot(patches, taps, preferred_element_type=f32).astype(bf16)
        for n in range(2):
            for h in range(SIDE):
                at = n * OUT + h * 16
                out_ref[n, h, :, cols] = back[at : at + SIDE]


def reduce_kernel(part_ref, mean_ref, square_ref, master_ref, out_ref):
    total = part_ref[0].astype(f32)
    for i in range(1, 64):
        total = total + part_ref[i].astype(f32)
    for i in range(4):
        for k in range(TILES):
            out_ref[i, 4 * k : 4 * k + 4, :] = total[k]
        for k in range(3):
            out_ref[i, 33 + 7 * k : 34 + 7 * k, :] = jnp.zeros((1, CG), f32)
    for k, ref in enumerate((mean_ref, square_ref, master_ref)):
        for row in range(7):
            at = USED + 7 * k + row
            some = min(CG, SHARD - row * CG)
            values = ref[pl.ds(row * CG, some)].reshape(1, some)
            for i in range(4):
                out_ref[i, at : at + 1, 0:some] = values


def adam(moment_mean, moment_square, master, grad):
    mean_next = 0.9 * moment_mean + 0.1 * grad
    square_next = 0.999 * moment_square + 0.001 * grad * grad
    fix_mean = 1.0 - 0.9**ADAM_STEP
    fix_square = 1.0 - 0.999**ADAM_STEP
    update = mean_next / fix_mean / (jnp.sqrt(square_next / fix_square) + 1e-08)
    return mean_next, square_next, master - 0.02 * update


def adam_kernel(in_ref, gain_ref, grad_ref, send_ref, frame):
    lane = lax.broadcasted_iota(jnp.int32, (7, CG), 1)
    frame[...] = jnp.zeros_like(frame)
    for p in range(4):
        base, shift = divmod(p * SHARD, CG)
        for k in range(3):
            rows = in_ref[p, USED + 7 * k : USED + 7 + 7 * k, :]
            if shift:
                rows = pltpu.roll(rows, shift, 1)
            frame[k, base : base + 7, :] += jnp.where(lane >= shift, rows, 0.0)
            if shift:
                frame[k, base + 1 : base + 8, :] += jnp.where(lane < shift, rows, 0.0)
    grad = (in_ref[0, 0:28, :] + in_ref[1, 0:28, :]) + (in_ref[2, 0:28, :] + in_ref[3, 0:28, :])
    grad_ref[0:28, :] = grad
    grad_ref[28:32, :] = jnp.zeros((4, CG), f32)
    master = adam(frame[0, 0:28, :], frame[1, 0:28, :], frame[2, 0:28, :], grad)[2]
    row = lax.broadcasted_iota(jnp.int32, (28, CG), 0)
    index = lax.broadcasted_iota(jnp.int32, (3, CG), 0) * CG + lax.broadcasted_iota(jnp.int32, (3, CG), 1)
    block = (lax.axis_index("z") * 4 + lax.axis_index("yh")) * 4 + lax.axis_index("co") * 2 + lax.axis_index("yl")
    mean_of = jnp.zeros((28, CG), f32)
    scale_of = jnp.zeros((28, CG), f32)
    for r in range(3):
        mine = (row >= 9 * r) & (row < 9 * r + 9)
        values = jnp.where(mine, master, 0.0)
        mean = jnp.sum(jnp.sum(values, 0, keepdims=True), 1, keepdims=True) / FAN
        square = jnp.sum(jnp.sum(values * values, 0, keepdims=True), 1, keepdims=True) / FAN
        picked = jnp.where(index == block * 3 + r, gain_ref[...], 0.0)
        gain = jnp.sum(jnp.sum(picked, 0, keepdims=True), 1, keepdims=True)
        scale = gain / jnp.sqrt(FAN * (square - mean * mean) + 0.0001)
        mean_of = jnp.where(mine, mean, mean_of)
        scale_of = jnp.where(mine, scale, scale_of)
    out = (master - mean_of) * scale_of
    for k in range(TILES):
        tile = out[4 * k : 4 * k + 4].astype(bf16)
        for i in range(64):
            send_ref[i, k] = tile


def assemble_kernel(own_ref, got_ref, out_ref, blocks, taps, rows, sems):
    me = lax.axis_index("co")
    for core in range(2):

        @pl.when(me == core)
        def _():
            for q in range(64):
                kept = (q // 2 * 4 + 2 * core + q % 2) * USED
                given = (q // 2 * 4 + 2 - 2 * core + q % 2) * USED
                for k in range(TILES):
                    at, some = 4 * k, min(4, USED - 4 * k)
                    blocks[kept + at : kept + at + some, :] = own_ref[q, k].astype(f32)[:some]
                    blocks[given + at : given + at + some, :] = got_ref[q, k].astype(f32)[:some]

    copies = []
    for part in range(3):
        for t in range(3 * part, 3 * part + 3):
            for r in range(3):
                taps[t, pl.ds(r, BLOCKS, 3), :] = blocks[pl.ds(9 * r + t, BLOCKS, USED), :]
            rows[part, :, (t - 3 * part) * CG : (t - 3 * part + 1) * CG] = taps[t].astype(bf16)
        cols = pl.ds(part * 3 * CG, 3 * CG)
        copies.append(pltpu.make_async_copy(rows.at[part], out_ref.at[:, cols], sems.at[part]))
        copies[-1].start()
    for copy in copies:
        copy.wait()


def shape(dims, dtype):
    return jax.ShapeDtypeStruct(dims, dtype)


def swap_cores(x):
    return lax.ppermute(x, "co", [(0, 1), (1, 0)])


def exchange(x, axes):
    return lax.all_to_all(x, axes, 0, 0, tiled=True)


def on_device(
    activations, cotangent, kernel, channel_gain, master_flat, moment_mean, moment_square
):
    pre_grad, keep, give = pl.pallas_call(
        grads_kernel,
        out_shape=(
            shape((2 * IMG, CMID), bf16),
            shape((64, TILES, 4, CG), bf16),
            shape((64, TILES, 4, CG), bf16),
        ),
        in_specs=[VMEM] * 3,
        out_specs=(VMEM,) * 3,
        scratch_shapes=[
            pltpu.VMEM((2 * IMG, CMID), f32),
            pltpu.VMEM((3, 2 * IMG, CMID), bf16),
            pltpu.VMEM((2 * OUT, CMID), f32),
            pltpu.VMEM((9, CMID, CG), f32),
            pltpu.VMEM((BLOCKS * USED + 8, CG), f32),
        ],
        compiler_params=grant(20),
        name="grads",
    )(activations, cotangent, kernel)
    got = swap_cores(give)
    input_grad = pl.pallas_call(
        input_kernel,
        out_shape=shape((2, SIDE, SIDE, CMID), bf16),
        in_specs=[VMEM] * 2,
        out_specs=VMEM,
        scratch_shapes=[pltpu.VMEM((3, 2 * IMG, CMID), bf16)],
        compiler_params=grant(12),
        name="input_grad",
    )(pre_grad, kernel)
    pair = (keep.astype(f32) + got.astype(f32)).astype(bf16)
    pair, input_grad = lax.optimization_barrier((pair, input_grad))
    parts = exchange(pair, ZY)
    payload = pl.pallas_call(
        reduce_kernel,
        out_shape=shape((4, 48, CG), f32),
        in_specs=[VMEM] * 4,
        out_specs=VMEM,
        compiler_params=grant(4),
        name="reduce",
    )(parts, moment_mean, moment_square, master_flat)
    gathered = exchange(payload, "x")
    grad, send = pl.pallas_call(
        adam_kernel,
        out_shape=(shape((ROWS, CG), f32), shape((64, TILES, 4, CG), bf16)),
        in_specs=[VMEM, VMEM],
        out_specs=(VMEM,) * 2,
        scratch_shapes=[pltpu.VMEM((3, 40, CG), f32)],
        compiler_params=grant(4),
        name="adam",
    )(gathered, channel_gain.reshape(3, CG))
    own = exchange(send, ZY)
    other = swap_cores(own)
    grad_shard = lax.dynamic_slice(
        grad.reshape(ROWS * CG), (lax.axis_index("x") * SHARD,), (SHARD,)
    )
    mean_next, square_next, master_next = adam(
        moment_mean, moment_square, master_flat, grad_shard
    )
    kernel_next = pl.pallas_call(
        assemble_kernel,
        out_shape=shape((CMID, FAN), bf16),
        in_specs=[VMEM] * 2,
        out_specs=pl.BlockSpec(memory_space=pl.ANY),
        scratch_shapes=[
            pltpu.VMEM((BLOCKS * USED + 8, CG), f32),
            pltpu.VMEM((9, CMID, CG), f32),
            pltpu.VMEM((3, CMID, 3 * CG), bf16),
            pltpu.SemaphoreType.DMA((3,)),
        ],
        compiler_params=grant(10),
        name="assemble",
    )(own, other)
    return (input_grad, master_next, mean_next, square_next, kernel_next)


def solution(mesh):
    fine = Mesh(mesh.devices.reshape(SIZES), AXES)
    images = P(AXES, None, None, None)
    state = P(AXES)
    return jax.shard_map(
        on_device,
        mesh=fine,
        in_specs=(images, images, P(), P(), state, state, state),
        out_specs=(images, state, state, state, P()),
        check_vma=False,
    )
```

```python
import jax
import jax.numpy as jnp
from jax import lax
from jax.experimental import pallas as pl
from jax.experimental.pallas import tpu as pltpu
from jax.sharding import Mesh, PartitionSpec as P

CMID = 384
CG = 128
ADAM_STEP = 10
GROUPS = 3
FAN = 1152
SIDE = 14
SHARD = 864
HALF_ROOT = 0.7071067811865476
INV_ROOT_TAU = 0.3989422804014327
bf16 = jnp.bfloat16
f32 = jnp.float32

AXES = ("z", "yh", "co", "yl", "x")
SIZES = (8, 4, 2, 2, 4)
ZY = ("z", "yh", "yl")
BLOCKS = CMID // 3
USED = 27
ROWS = 32
TILES = 7
IMG = 256
OUT = SIDE * 16
VMEM = pl.BlockSpec(memory_space=pltpu.VMEM)


def grant(mib):
    return pltpu.CompilerParams(vmem_limit_bytes=mib * 2**20)


def gelu_slope(values):
    return (
        0.5 * (1.0 + lax.erf(values * HALF_ROOT))
        + values * jnp.exp(-0.5 * values * values) * INV_ROOT_TAU
    )


def shift_columns(full, shifted):
    shifted[0] = pltpu.roll(full, 1, 0).astype(bf16)
    shifted[1] = full.astype(bf16)
    shifted[2] = pltpu.roll(full, full.shape[0] - 1, 0).astype(bf16)


def window(shifted, cols, row_off, col_off):
    return jnp.concatenate(
        [shifted[col_off, n * IMG + row_off * 16 : n * IMG + row_off * 16 + OUT, cols] for n in range(2)],
        0,
    )


def widen(cells):
    return jnp.concatenate([cells.astype(f32), jnp.zeros((2, CMID), f32)], 0)


def grads_kernel(x_ref, cot_ref, k_ref, pg_ref, blocks, give_ref, xf, xs, cf, taps):
    me = lax.axis_index("co")
    for n in range(2):
        for at in (n * IMG, n * IMG + 240):
            xf[at : at + 16, :] = jnp.zeros((16, CMID), f32)
            pg_ref[at : at + 16, :] = jnp.zeros((16, CMID), bf16)
        for h in range(SIDE):
            at = n * IMG + (h + 1) * 16
            xf[at : at + 16, :] = widen(x_ref[n, h])
            at = n * OUT + h * 16
            cf[at : at + 16, :] = widen(cot_ref[n, h])
    shift_columns(xf[...], xs)
    def group(g):
        cols = slice(g * CG, (g + 1) * CG)
        return cols, jnp.concatenate([window(xs, cols, t // 3, t % 3) for t in range(9)], 1)

    def forward(g):
        cols, patches = group(g)
        return lax.dot_general(
            patches, k_ref[cols, :], (((1,), (1,)), ((), ())), preferred_element_type=f32
        )

    def slope(g, pre):
        cols = slice(g * CG, (g + 1) * CG)
        pg = (cf[:, cols] * gelu_slope(pre)).astype(bf16)
        for n in range(2):
            pg_ref[n * IMG + 16 : n * IMG + 16 + OUT, cols] = pg[n * OUT : (n + 1) * OUT]
        return pg

    def weight(g, pg):
        cols, patches = group(g)
        grad = lax.dot_general(pg, patches, (((0,), (0,)), ((), ())), preferred_element_type=f32)
        for t in range(9):
            taps[t, cols, :] = grad[:, t * CG : (t + 1) * CG]

    pre = [forward(g) for g in range(GROUPS)]
    for g in range(GROUPS):
        weight(g, slope(g, pre[g]))
    for t in range(9):
        for r in range(3):
            blocks[pl.ds(9 * r + t, BLOCKS, USED), :] = taps[t, pl.ds(r, BLOCKS, 3), :]
    blocks[BLOCKS * USED :, :] = jnp.zeros((8, CG), f32)
    for core in range(2):

        @pl.when(me == core)
        def _():
            for q in range(64):
                given = (q // 2 * 4 + 2 - 2 * core + q % 2) * USED
                for k in range(TILES):
                    at = given + 4 * k
                    give_ref[q, k] = blocks[at : at + 4, :].astype(bf16)


def input_kernel(pg_ref, k_ref, blocks, out_ref, keep_ref, ps):
    me = lax.axis_index("co")
    for core in range(2):

        @pl.when(me == core)
        def _():
            for q in range(64):
                kept = (q // 2 * 4 + 2 * core + q % 2) * USED
                for k in range(TILES):
                    at = kept + 4 * k
                    keep_ref[q, k] = blocks[at : at + 4, :].astype(bf16)

    shift_columns(pg_ref[...].astype(f32), ps)
    for g in range(GROUPS):
        cols = slice(g * CG, (g + 1) * CG)
        patches = jnp.concatenate([window(ps, cols, 2 - t // 3, 2 - t % 3) for t in range(9)], 1)
        taps = jnp.concatenate([k_ref[cols, t * CG : (t + 1) * CG] for t in range(9)], 0)
        back = jnp.dot(patches, taps, preferred_element_type=f32).astype(bf16)
        for n in range(2):
            for h in range(SIDE):
                at = n * OUT + h * 16
                out_ref[n, h, :, cols] = back[at : at + SIDE]


def reduce_kernel(part_ref, mean_ref, square_ref, master_ref, out_ref):
    total = part_ref[0].astype(f32)
    for i in range(1, 64):
        total = total + part_ref[i].astype(f32)
    for i in range(4):
        for k in range(TILES):
            out_ref[i, 4 * k : 4 * k + 4, :] = total[k]
        for k in range(3):
            out_ref[i, 33 + 7 * k : 34 + 7 * k, :] = jnp.zeros((1, CG), f32)
    for k, ref in enumerate((mean_ref, square_ref, master_ref)):
        for row in range(7):
            at = USED + 7 * k + row
            some = min(CG, SHARD - row * CG)
            values = ref[pl.ds(row * CG, some)].reshape(1, some)
            for i in range(4):
                out_ref[i, at : at + 1, 0:some] = values


def adam(moment_mean, moment_square, master, grad):
    mean_next = 0.9 * moment_mean + 0.1 * grad
    square_next = 0.999 * moment_square + 0.001 * grad * grad
    fix_mean = 1.0 - 0.9**ADAM_STEP
    fix_square = 1.0 - 0.999**ADAM_STEP
    update = mean_next / fix_mean / (jnp.sqrt(square_next / fix_square) + 1e-08)
    return mean_next, square_next, master - 0.02 * update


def adam_kernel(in_ref, gain_ref, grad_ref, send_ref, frame):
    lane = lax.broadcasted_iota(jnp.int32, (7, CG), 1)
    frame[...] = jnp.zeros_like(frame)
    for p in range(4):
        base, shift = divmod(p * SHARD, CG)
        for k in range(3):
            rows = in_ref[p, USED + 7 * k : USED + 7 + 7 * k, :]
            if shift:
                rows = pltpu.roll(rows, shift, 1)
            frame[k, base : base + 7, :] += jnp.where(lane >= shift, rows, 0.0)
            if shift:
                frame[k, base + 1 : base + 8, :] += jnp.where(lane < shift, rows, 0.0)
    grad = (in_ref[0, 0:28, :] + in_ref[1, 0:28, :]) + (in_ref[2, 0:28, :] + in_ref[3, 0:28, :])
    grad_ref[0:28, :] = grad
    grad_ref[28:32, :] = jnp.zeros((4, CG), f32)
    master = adam(frame[0, 0:28, :], frame[1, 0:28, :], frame[2, 0:28, :], grad)[2]
    row = lax.broadcasted_iota(jnp.int32, (28, CG), 0)
    index = lax.broadcasted_iota(jnp.int32, (3, CG), 0) * CG + lax.broadcasted_iota(jnp.int32, (3, CG), 1)
    block = (lax.axis_index("z") * 4 + lax.axis_index("yh")) * 4 + lax.axis_index("co") * 2 + lax.axis_index("yl")
    mean_of = jnp.zeros((28, CG), f32)
    scale_of = jnp.zeros((28, CG), f32)
    for r in range(3):
        mine = (row >= 9 * r) & (row < 9 * r + 9)
        values = jnp.where(mine, master, 0.0)
        mean = jnp.sum(jnp.sum(values, 0, keepdims=True), 1, keepdims=True) / FAN
        square = jnp.sum(jnp.sum(values * values, 0, keepdims=True), 1, keepdims=True) / FAN
        picked = jnp.where(index == block * 3 + r, gain_ref[...], 0.0)
        gain = jnp.sum(jnp.sum(picked, 0, keepdims=True), 1, keepdims=True)
        scale = gain / jnp.sqrt(FAN * (square - mean * mean) + 0.0001)
        mean_of = jnp.where(mine, mean, mean_of)
        scale_of = jnp.where(mine, scale, scale_of)
    out = (master - mean_of) * scale_of
    for k in range(TILES):
        tile = out[4 * k : 4 * k + 4].astype(bf16)
        for i in range(64):
            send_ref[i, k] = tile


def assemble_kernel(own_ref, got_ref, out_ref, blocks, taps, rows, sems):
    me = lax.axis_index("co")
    for core in range(2):

        @pl.when(me == core)
        def _():
            for q in range(64):
                kept = (q // 2 * 4 + 2 * core + q % 2) * USED
                given = (q // 2 * 4 + 2 - 2 * core + q % 2) * USED
                for k in range(TILES):
                    at, some = 4 * k, min(4, USED - 4 * k)
                    blocks[kept + at : kept + at + some, :] = own_ref[q, k].astype(f32)[:some]
                    blocks[given + at : given + at + some, :] = got_ref[q, k].astype(f32)[:some]

    copies = []
    for t in range(9):
        for r in range(3):
            taps[t, pl.ds(r, BLOCKS, 3), :] = blocks[pl.ds(9 * r + t, BLOCKS, USED), :]
        rows[t] = taps[t].astype(bf16)
        cols = pl.ds(t * CG, CG)
        copies.append(pltpu.make_async_copy(rows.at[t], out_ref.at[:, cols], sems.at[t]))
        copies[-1].start()
    for copy in copies:
        copy.wait()


def shape(dims, dtype):
    return jax.ShapeDtypeStruct(dims, dtype)


def swap_cores(x):
    return lax.ppermute(x, "co", [(0, 1), (1, 0)])


def exchange(x, axes):
    return lax.all_to_all(x, axes, 0, 0, tiled=True)


def on_device(
    activations, cotangent, kernel, channel_gain, master_flat, moment_mean, moment_square
):
    pre_grad, blocks, give = pl.pallas_call(
        grads_kernel,
        out_shape=(
            shape((2 * IMG, CMID), bf16),
            shape((BLOCKS * USED + 8, CG), f32),
            shape((64, TILES, 4, CG), bf16),
        ),
        in_specs=[VMEM] * 3,
        out_specs=(VMEM,) * 3,
        scratch_shapes=[
            pltpu.VMEM((2 * IMG, CMID), f32),
            pltpu.VMEM((3, 2 * IMG, CMID), bf16),
            pltpu.VMEM((2 * OUT, CMID), f32),
            pltpu.VMEM((9, CMID, CG), f32),
        ],
        compiler_params=grant(20),
        name="grads",
    )(activations, cotangent, kernel)
    got = swap_cores(give)
    input_grad, keep = pl.pallas_call(
        input_kernel,
        out_shape=(shape((2, SIDE, SIDE, CMID), bf16), shape((64, TILES, 4, CG), bf16)),
        in_specs=[VMEM] * 3,
        out_specs=(VMEM,) * 2,
        scratch_shapes=[pltpu.VMEM((3, 2 * IMG, CMID), bf16)],
        compiler_params=grant(12),
        name="input_grad",
    )(pre_grad, kernel, blocks)
    pair = (keep.astype(f32) + got.astype(f32)).astype(bf16)
    parts = exchange(pair, ZY)
    payload = pl.pallas_call(
        reduce_kernel,
        out_shape=shape((4, 48, CG), f32),
        in_specs=[VMEM] * 4,
        out_specs=VMEM,
        compiler_params=grant(4),
        name="reduce",
    )(parts, moment_mean, moment_square, master_flat)
    gathered = exchange(payload, "x")
    grad, send = pl.pallas_call(
        adam_kernel,
        out_shape=(shape((ROWS, CG), f32), shape((64, TILES, 4, CG), bf16)),
        in_specs=[VMEM, VMEM],
        out_specs=(VMEM,) * 2,
        scratch_shapes=[pltpu.VMEM((3, 40, CG), f32)],
        compiler_params=grant(4),
        name="adam",
    )(gathered, channel_gain.reshape(3, CG))
    own = exchange(send, ZY)
    other = swap_cores(own)
    grad_shard = lax.dynamic_slice(
        grad.reshape(ROWS * CG), (lax.axis_index("x") * SHARD,), (SHARD,)
    )
    mean_next, square_next, master_next = adam(
        moment_mean, moment_square, master_flat, grad_shard
    )
    kernel_next = pl.pallas_call(
        assemble_kernel,
        out_shape=shape((CMID, FAN), bf16),
        in_specs=[VMEM] * 2,
        out_specs=pl.BlockSpec(memory_space=pl.ANY),
        scratch_shapes=[
            pltpu.VMEM((BLOCKS * USED + 8, CG), f32),
            pltpu.VMEM((9, CMID, CG), f32),
            pltpu.VMEM((9, CMID, CG), bf16),
            pltpu.SemaphoreType.DMA((9,)),
        ],
        compiler_params=grant(10),
        name="assemble",
    )(own, other)
    return (input_grad, master_next, mean_next, square_next, kernel_next)


def solution(mesh):
    fine = Mesh(mesh.devices.reshape(SIZES), AXES)
    images = P(AXES, None, None, None)
    state = P(AXES)
    return jax.shard_map(
        on_device,
        mesh=fine,
        in_specs=(images, images, P(), P(), state, state, state),
        out_specs=(images, state, state, state, P()),
        check_vma=False,
    )
```

```python
import jax
import jax.numpy as jnp
from jax import lax
from jax.experimental import pallas as pl
from jax.experimental.pallas import tpu as pltpu
from jax.sharding import Mesh, PartitionSpec as P

CMID = 384
CG = 128
ADAM_STEP = 10
GROUPS = 3
FAN = 1152
SIDE = 14
SHARD = 864
HALF_ROOT = 0.7071067811865476
INV_ROOT_TAU = 0.3989422804014327
bf16 = jnp.bfloat16
f32 = jnp.float32

AXES = ("z", "yh", "co", "yl", "x")
SIZES = (8, 4, 2, 2, 4)
ZY = ("z", "yh", "yl")
BLOCKS = CMID // 3
USED = 27
ROWS = 32
TILES = 7
IMG = 256
OUT = SIDE * 16
VMEM = pl.BlockSpec(memory_space=pltpu.VMEM)


def grant(mib):
    return pltpu.CompilerParams(vmem_limit_bytes=mib * 2**20)


def gelu_slope(values):
    return (
        0.5 * (1.0 + lax.erf(values * HALF_ROOT))
        + values * jnp.exp(-0.5 * values * values) * INV_ROOT_TAU
    )


def shift_columns(full, shifted):
    shifted[0] = pltpu.roll(full, 1, 0).astype(bf16)
    shifted[1] = full.astype(bf16)
    shifted[2] = pltpu.roll(full, full.shape[0] - 1, 0).astype(bf16)


def window(shifted, cols, row_off, col_off):
    return jnp.concatenate(
        [shifted[col_off, n * IMG + row_off * 16 : n * IMG + row_off * 16 + OUT, cols] for n in range(2)],
        0,
    )


def widen(cells):
    return jnp.concatenate([cells.astype(f32), jnp.zeros((2, CMID), f32)], 0)


def grads_kernel(x_ref, cot_ref, k_ref, pg_ref, keep_ref, give_ref, xf, xs, cf, taps, blocks):
    me = lax.axis_index("co")
    for n in range(2):
        for at in (n * IMG, n * IMG + 240):
            xf[at : at + 16, :] = jnp.zeros((16, CMID), f32)
            pg_ref[at : at + 16, :] = jnp.zeros((16, CMID), bf16)
        for h in range(SIDE):
            at = n * IMG + (h + 1) * 16
            xf[at : at + 16, :] = widen(x_ref[n, h])
            at = n * OUT + h * 16
            cf[at : at + 16, :] = widen(cot_ref[n, h])
    shift_columns(xf[...], xs)
    def group(g):
        cols = slice(g * CG, (g + 1) * CG)
        return cols, jnp.concatenate([window(xs, cols, t // 3, t % 3) for t in range(9)], 1)

    def forward(g):
        cols, patches = group(g)
        return lax.dot_general(
            patches, k_ref[cols, :], (((1,), (1,)), ((), ())), preferred_element_type=f32
        )

    def slope(g, pre):
        cols = slice(g * CG, (g + 1) * CG)
        pg = (cf[:, cols] * gelu_slope(pre)).astype(bf16)
        for n in range(2):
            pg_ref[n * IMG + 16 : n * IMG + 16 + OUT, cols] = pg[n * OUT : (n + 1) * OUT]
        return pg

    def weight(g, pg):
        cols, patches = group(g)
        grad = lax.dot_general(pg, patches, (((0,), (0,)), ((), ())), preferred_element_type=f32)
        for t in range(9):
            taps[t, cols, :] = grad[:, t * CG : (t + 1) * CG]

    pre = [forward(g) for g in range(GROUPS)]
    for g in range(GROUPS):
        weight(g, slope(g, pre[g]))
    for t in range(9):
        for r in range(3):
            blocks[pl.ds(9 * r + t, BLOCKS, USED), :] = taps[t, pl.ds(r, BLOCKS, 3), :]
    blocks[BLOCKS * USED :, :] = jnp.zeros((8, CG), f32)
    for core in range(2):

        @pl.when(me == core)
        def _():
            for q in range(64):
                kept = (q // 2 * 4 + 2 * core + q % 2) * USED
                given = (q // 2 * 4 + 2 - 2 * core + q % 2) * USED
                for k in range(TILES):
                    at = 4 * k
                    keep_ref[q, k] = blocks[kept + at : kept + at + 4, :].astype(bf16)
                    give_ref[q, k] = blocks[given + at : given + at + 4, :].astype(bf16)


def input_kernel(pg_ref, k_ref, out_ref, ps):
    shift_columns(pg_ref[...].astype(f32), ps)
    for g in range(GROUPS):
        cols = slice(g * CG, (g + 1) * CG)
        patches = jnp.concatenate([window(ps, cols, 2 - t // 3, 2 - t % 3) for t in range(9)], 1)
        taps = jnp.concatenate([k_ref[cols, t * CG : (t + 1) * CG] for t in range(9)], 0)
        back = jnp.dot(patches, taps, preferred_element_type=f32).astype(bf16)
        for n in range(2):
            for h in range(SIDE):
                at = n * OUT + h * 16
                out_ref[n, h, :, cols] = back[at : at + SIDE]


def reduce_kernel(part_ref, mean_ref, square_ref, master_ref, out_ref):
    total = part_ref[0].astype(f32)
    for i in range(1, 64):
        total = total + part_ref[i].astype(f32)
    for i in range(4):
        for k in range(TILES):
            out_ref[i, 4 * k : 4 * k + 4, :] = total[k]
        for k in range(3):
            out_ref[i, 33 + 7 * k : 34 + 7 * k, :] = jnp.zeros((1, CG), f32)
    for k, ref in enumerate((mean_ref, square_ref, master_ref)):
        for row in range(7):
            at = USED + 7 * k + row
            some = min(CG, SHARD - row * CG)
            values = ref[pl.ds(row * CG, some)].reshape(1, some)
            for i in range(4):
                out_ref[i, at : at + 1, 0:some] = values


def adam(moment_mean, moment_square, master, grad):
    mean_next = 0.9 * moment_mean + 0.1 * grad
    square_next = 0.999 * moment_square + 0.001 * grad * grad
    fix_mean = 1.0 - 0.9**ADAM_STEP
    fix_square = 1.0 - 0.999**ADAM_STEP
    update = mean_next / fix_mean / (jnp.sqrt(square_next / fix_square) + 1e-08)
    return mean_next, square_next, master - 0.02 * update


def adam_kernel(in_ref, gain_ref, grad_ref, send_ref, frame):
    lane = lax.broadcasted_iota(jnp.int32, (7, CG), 1)
    frame[...] = jnp.zeros_like(frame)
    for p in range(4):
        base, shift = divmod(p * SHARD, CG)
        for k in range(3):
            rows = in_ref[p, USED + 7 * k : USED + 7 + 7 * k, :]
            if shift:
                rows = pltpu.roll(rows, shift, 1)
            frame[k, base : base + 7, :] += jnp.where(lane >= shift, rows, 0.0)
            if shift:
                frame[k, base + 1 : base + 8, :] += jnp.where(lane < shift, rows, 0.0)
    grad = (in_ref[0, 0:28, :] + in_ref[1, 0:28, :]) + (in_ref[2, 0:28, :] + in_ref[3, 0:28, :])
    grad_ref[0:28, :] = grad
    grad_ref[28:32, :] = jnp.zeros((4, CG), f32)
    master = adam(frame[0, 0:28, :], frame[1, 0:28, :], frame[2, 0:28, :], grad)[2]
    row = lax.broadcasted_iota(jnp.int32, (28, CG), 0)
    index = lax.broadcasted_iota(jnp.int32, (3, CG), 0) * CG + lax.broadcasted_iota(jnp.int32, (3, CG), 1)
    block = (lax.axis_index("z") * 4 + lax.axis_index("yh")) * 4 + lax.axis_index("co") * 2 + lax.axis_index("yl")
    mean_of = jnp.zeros((28, CG), f32)
    scale_of = jnp.zeros((28, CG), f32)
    for r in range(3):
        mine = (row >= 9 * r) & (row < 9 * r + 9)
        values = jnp.where(mine, master, 0.0)
        mean = jnp.sum(jnp.sum(values, 0, keepdims=True), 1, keepdims=True) / FAN
        square = jnp.sum(jnp.sum(values * values, 0, keepdims=True), 1, keepdims=True) / FAN
        picked = jnp.where(index == block * 3 + r, gain_ref[...], 0.0)
        gain = jnp.sum(jnp.sum(picked, 0, keepdims=True), 1, keepdims=True)
        scale = gain / jnp.sqrt(FAN * (square - mean * mean) + 0.0001)
        mean_of = jnp.where(mine, mean, mean_of)
        scale_of = jnp.where(mine, scale, scale_of)
    out = (master - mean_of) * scale_of
    for k in range(TILES):
        tile = out[4 * k : 4 * k + 4].astype(bf16)
        for i in range(64):
            send_ref[i, k] = tile


def assemble_kernel(own_ref, got_ref, out_ref, blocks, taps, rows, sems):
    me = lax.axis_index("co")
    for core in range(2):

        @pl.when(me == core)
        def _():
            for q in range(64):
                kept = (q // 2 * 4 + 2 * core + q % 2) * USED
                given = (q // 2 * 4 + 2 - 2 * core + q % 2) * USED
                for k in range(TILES):
                    at, some = 4 * k, min(4, USED - 4 * k)
                    blocks[kept + at : kept + at + some, :] = own_ref[q, k].astype(f32)[:some]
                    blocks[given + at : given + at + some, :] = got_ref[q, k].astype(f32)[:some]

    copies = []
    for t in range(9):
        for r in range(3):
            taps[t, pl.ds(r, BLOCKS, 3), :] = blocks[pl.ds(9 * r + t, BLOCKS, USED), :]
        rows[t] = taps[t].astype(bf16)
        cols = pl.ds(t * CG, CG)
        copies.append(pltpu.make_async_copy(rows.at[t], out_ref.at[:, cols], sems.at[t]))
        copies[-1].start()
    for copy in copies:
        copy.wait()


def shape(dims, dtype):
    return jax.ShapeDtypeStruct(dims, dtype)


def swap_cores(x):
    return lax.ppermute(x, "co", [(0, 1), (1, 0)])


def exchange(x, axes):
    return lax.all_to_all(x, axes, 0, 0, tiled=True)


def on_device(
    activations, cotangent, kernel, channel_gain, master_flat, moment_mean, moment_square
):
    pre_grad, keep, give = pl.pallas_call(
        grads_kernel,
        out_shape=(
            shape((2 * IMG, CMID), bf16),
            shape((64, TILES, 4, CG), bf16),
            shape((64, TILES, 4, CG), bf16),
        ),
        in_specs=[VMEM] * 3,
        out_specs=(VMEM,) * 3,
        scratch_shapes=[
            pltpu.VMEM((2 * IMG, CMID), f32),
            pltpu.VMEM((3, 2 * IMG, CMID), bf16),
            pltpu.VMEM((2 * OUT, CMID), f32),
            pltpu.VMEM((9, CMID, CG), f32),
            pltpu.VMEM((BLOCKS * USED + 8, CG), f32),
        ],
        compiler_params=grant(20),
        name="grads",
    )(activations, cotangent, kernel)
    got = swap_cores(give)
    input_grad = pl.pallas_call(
        input_kernel,
        out_shape=shape((2, SIDE, SIDE, CMID), bf16),
        in_specs=[VMEM] * 2,
        out_specs=VMEM,
        scratch_shapes=[pltpu.VMEM((3, 2 * IMG, CMID), bf16)],
        compiler_params=grant(12),
        name="input_grad",
    )(pre_grad, kernel)
    pair = (keep.astype(f32) + got.astype(f32)).astype(bf16)
    pair, input_grad = lax.optimization_barrier((pair, input_grad))
    parts = exchange(pair, ZY)
    payload = pl.pallas_call(
        reduce_kernel,
        out_shape=shape((4, 48, CG), f32),
        in_specs=[VMEM] * 4,
        out_specs=VMEM,
        compiler_params=grant(4),
        name="reduce",
    )(parts, moment_mean, moment_square, master_flat)
    gathered = exchange(payload, "x")
    grad, send = pl.pallas_call(
        adam_kernel,
        out_shape=(shape((ROWS, CG), f32), shape((64, TILES, 4, CG), bf16)),
        in_specs=[VMEM, VMEM],
        out_specs=(VMEM,) * 2,
        scratch_shapes=[pltpu.VMEM((3, 40, CG), f32)],
        compiler_params=grant(4),
        name="adam",
    )(gathered, channel_gain.reshape(3, CG))
    own = exchange(send, ZY)
    other = swap_cores(own)
    grad_shard = lax.dynamic_slice(
        grad.reshape(ROWS * CG), (lax.axis_index("x") * SHARD,), (SHARD,)
    )
    mean_next, square_next, master_next = adam(
        moment_mean, moment_square, master_flat, grad_shard
    )
    kernel_next = pl.pallas_call(
        assemble_kernel,
        out_shape=shape((CMID, FAN), bf16),
        in_specs=[VMEM] * 2,
        out_specs=pl.BlockSpec(memory_space=pl.ANY),
        scratch_shapes=[
            pltpu.VMEM((BLOCKS * USED + 8, CG), f32),
            pltpu.VMEM((9, CMID, CG), f32),
            pltpu.VMEM((9, CMID, CG), bf16),
            pltpu.SemaphoreType.DMA((9,)),
        ],
        compiler_params=grant(10),
        name="assemble",
    )(own, other)
    return (input_grad, master_next, mean_next, square_next, kernel_next)


def solution(mesh):
    fine = Mesh(mesh.devices.reshape(SIZES), AXES)
    images = P(AXES, None, None, None)
    state = P(AXES)
    return jax.shard_map(
        on_device,
        mesh=fine,
        in_specs=(images, images, P(), P(), state, state, state),
        out_specs=(images, state, state, state, P()),
        check_vma=False,
    )
```

```python
import jax
import jax.numpy as jnp
from jax import lax
from jax.experimental import pallas as pl
from jax.experimental.pallas import tpu as pltpu
from jax.sharding import Mesh, PartitionSpec as P

CMID = 384
CG = 128
ADAM_STEP = 10
GROUPS = 3
FAN = 1152
SIDE = 14
SHARD = 864
HALF_ROOT = 0.7071067811865476
INV_ROOT_TAU = 0.3989422804014327
bf16 = jnp.bfloat16
f32 = jnp.float32

AXES = ("z", "yh", "co", "yl", "x")
SIZES = (8, 4, 2, 2, 4)
ZY = ("z", "yh", "yl")
BLOCKS = CMID // 3
USED = 27
ROWS = 32
TILES = 7
IMG = 256
OUT = SIDE * 16
VMEM = pl.BlockSpec(memory_space=pltpu.VMEM)


def grant(mib):
    return pltpu.CompilerParams(vmem_limit_bytes=mib * 2**20)


def gelu_slope(values):
    return (
        0.5 * (1.0 + lax.erf(values * HALF_ROOT))
        + values * jnp.exp(-0.5 * values * values) * INV_ROOT_TAU
    )


def shift_columns(full, shifted):
    shifted[0] = pltpu.roll(full, 1, 0).astype(bf16)
    shifted[1] = full.astype(bf16)
    shifted[2] = pltpu.roll(full, full.shape[0] - 1, 0).astype(bf16)


def window(shifted, cols, row_off, col_off):
    return jnp.concatenate(
        [shifted[col_off, n * IMG + row_off * 16 : n * IMG + row_off * 16 + OUT, cols] for n in range(2)],
        0,
    )


def widen(cells):
    return jnp.concatenate([cells.astype(f32), jnp.zeros((2, CMID), f32)], 0)


def grads_kernel(x_ref, cot_ref, k_ref, pg_ref, keep_ref, give_ref, xf, xs, cf, taps, blocks):
    me = lax.axis_index("co")
    for n in range(2):
        for at in (n * IMG, n * IMG + 240):
            xf[at : at + 16, :] = jnp.zeros((16, CMID), f32)
            pg_ref[at : at + 16, :] = jnp.zeros((16, CMID), bf16)
        for h in range(SIDE):
            at = n * IMG + (h + 1) * 16
            xf[at : at + 16, :] = widen(x_ref[n, h])
            at = n * OUT + h * 16
            cf[at : at + 16, :] = widen(cot_ref[n, h])
    shift_columns(xf[...], xs)
    def group(g):
        cols = slice(g * CG, (g + 1) * CG)
        return cols, jnp.concatenate([window(xs, cols, t // 3, t % 3) for t in range(9)], 1)

    def forward(g):
        cols, patches = group(g)
        return lax.dot_general(
            patches, k_ref[cols, :], (((1,), (1,)), ((), ())), preferred_element_type=f32
        )

    def slope(g, pre):
        cols = slice(g * CG, (g + 1) * CG)
        pg = (cf[:, cols] * gelu_slope(pre)).astype(bf16)
        for n in range(2):
            pg_ref[n * IMG + 16 : n * IMG + 16 + OUT, cols] = pg[n * OUT : (n + 1) * OUT]
        return pg

    def weight(g, pg):
        cols, patches = group(g)
        grad = lax.dot_general(pg, patches, (((0,), (0,)), ((), ())), preferred_element_type=f32)
        for t in range(9):
            taps[t, cols, :] = grad[:, t * CG : (t + 1) * CG]

    pre = [forward(g) for g in range(GROUPS)]
    for g in range(GROUPS):
        weight(g, slope(g, pre[g]))
    for t in range(9):
        for r in range(3):
            blocks[pl.ds(9 * r + t, BLOCKS, USED), :] = taps[t, pl.ds(r, BLOCKS, 3), :]
    blocks[BLOCKS * USED :, :] = jnp.zeros((8, CG), f32)
    for core in range(2):

        @pl.when(me == core)
        def _():
            for q in range(64):
                kept = (q // 2 * 4 + 2 * core + q % 2) * USED
                given = (q // 2 * 4 + 2 - 2 * core + q % 2) * USED
                for k in range(TILES):
                    at = 4 * k
                    keep_ref[q, k] = blocks[kept + at : kept + at + 4, :].astype(bf16)
                    give_ref[q, k] = blocks[given + at : given + at + 4, :].astype(bf16)


def input_kernel(pg_ref, k_ref, out_ref, ps):
    shift_columns(pg_ref[...].astype(f32), ps)
    for g in range(GROUPS):
        cols = slice(g * CG, (g + 1) * CG)
        patches = jnp.concatenate([window(ps, cols, 2 - t // 3, 2 - t % 3) for t in range(9)], 1)
        taps = jnp.concatenate([k_ref[cols, t * CG : (t + 1) * CG] for t in range(9)], 0)
        back = jnp.dot(patches, taps, preferred_element_type=f32).astype(bf16)
        for n in range(2):
            for h in range(SIDE):
                at = n * OUT + h * 16
                out_ref[n, h, :, cols] = back[at : at + SIDE]


def reduce_kernel(part_ref, mean_ref, square_ref, master_ref, out_ref):
    sums = [part_ref[i].astype(f32) for i in range(4)]
    for i in range(4, 64):
        sums[i % 4] = sums[i % 4] + part_ref[i].astype(f32)
    total = (sums[0] + sums[1]) + (sums[2] + sums[3])
    for i in range(4):
        for k in range(TILES):
            out_ref[i, 4 * k : 4 * k + 4, :] = total[k]
        for k in range(3):
            out_ref[i, 33 + 7 * k : 34 + 7 * k, :] = jnp.zeros((1, CG), f32)
    for k, ref in enumerate((mean_ref, square_ref, master_ref)):
        for row in range(7):
            at = USED + 7 * k + row
            some = min(CG, SHARD - row * CG)
            values = ref[pl.ds(row * CG, some)].reshape(1, some)
            for i in range(4):
                out_ref[i, at : at + 1, 0:some] = values


def adam(moment_mean, moment_square, master, grad):
    mean_next = 0.9 * moment_mean + 0.1 * grad
    square_next = 0.999 * moment_square + 0.001 * grad * grad
    fix_mean = 1.0 - 0.9**ADAM_STEP
    fix_square = 1.0 - 0.999**ADAM_STEP
    update = mean_next / fix_mean / (jnp.sqrt(square_next / fix_square) + 1e-08)
    return mean_next, square_next, master - 0.02 * update


def adam_kernel(in_ref, gain_ref, grad_ref, send_ref, frame):
    lane = lax.broadcasted_iota(jnp.int32, (7, CG), 1)
    frame[...] = jnp.zeros_like(frame)
    for p in range(4):
        base, shift = divmod(p * SHARD, CG)
        for k in range(3):
            rows = in_ref[p, USED + 7 * k : USED + 7 + 7 * k, :]
            if shift:
                rows = pltpu.roll(rows, shift, 1)
            frame[k, base : base + 7, :] += jnp.where(lane >= shift, rows, 0.0)
            if shift:
                frame[k, base + 1 : base + 8, :] += jnp.where(lane < shift, rows, 0.0)
    grad = (in_ref[0, 0:28, :] + in_ref[1, 0:28, :]) + (in_ref[2, 0:28, :] + in_ref[3, 0:28, :])
    grad_ref[0:28, :] = grad
    grad_ref[28:32, :] = jnp.zeros((4, CG), f32)
    master = adam(frame[0, 0:28, :], frame[1, 0:28, :], frame[2, 0:28, :], grad)[2]
    row = lax.broadcasted_iota(jnp.int32, (28, CG), 0)
    index = lax.broadcasted_iota(jnp.int32, (3, CG), 0) * CG + lax.broadcasted_iota(jnp.int32, (3, CG), 1)
    block = (lax.axis_index("z") * 4 + lax.axis_index("yh")) * 4 + lax.axis_index("co") * 2 + lax.axis_index("yl")
    mean_of = jnp.zeros((28, CG), f32)
    scale_of = jnp.zeros((28, CG), f32)
    for r in range(3):
        mine = (row >= 9 * r) & (row < 9 * r + 9)
        values = jnp.where(mine, master, 0.0)
        mean = jnp.sum(jnp.sum(values, 0, keepdims=True), 1, keepdims=True) / FAN
        square = jnp.sum(jnp.sum(values * values, 0, keepdims=True), 1, keepdims=True) / FAN
        picked = jnp.where(index == block * 3 + r, gain_ref[...], 0.0)
        gain = jnp.sum(jnp.sum(picked, 0, keepdims=True), 1, keepdims=True)
        scale = gain / jnp.sqrt(FAN * (square - mean * mean) + 0.0001)
        mean_of = jnp.where(mine, mean, mean_of)
        scale_of = jnp.where(mine, scale, scale_of)
    out = (master - mean_of) * scale_of
    for k in range(TILES):
        tile = out[4 * k : 4 * k + 4].astype(bf16)
        for i in range(64):
            send_ref[i, k] = tile


def assemble_kernel(own_ref, got_ref, out_ref, blocks, taps, rows, sems):
    me = lax.axis_index("co")
    for core in range(2):

        @pl.when(me == core)
        def _():
            for q in range(64):
                kept = (q // 2 * 4 + 2 * core + q % 2) * USED
                given = (q // 2 * 4 + 2 - 2 * core + q % 2) * USED
                for k in range(TILES):
                    at, some = 4 * k, min(4, USED - 4 * k)
                    blocks[kept + at : kept + at + some, :] = own_ref[q, k].astype(f32)[:some]
                    blocks[given + at : given + at + some, :] = got_ref[q, k].astype(f32)[:some]

    copies = []
    for part in range(3):
        for t in range(3 * part, 3 * part + 3):
            for r in range(3):
                taps[t, pl.ds(r, BLOCKS, 3), :] = blocks[pl.ds(9 * r + t, BLOCKS, USED), :]
            rows[part, :, (t - 3 * part) * CG : (t - 3 * part + 1) * CG] = taps[t].astype(bf16)
        cols = pl.ds(part * 3 * CG, 3 * CG)
        copies.append(pltpu.make_async_copy(rows.at[part], out_ref.at[:, cols], sems.at[part]))
        copies[-1].start()
    for copy in copies:
        copy.wait()


def shape(dims, dtype):
    return jax.ShapeDtypeStruct(dims, dtype)


def swap_cores(x):
    return lax.ppermute(x, "co", [(0, 1), (1, 0)])


def exchange(x, axes):
    return lax.all_to_all(x, axes, 0, 0, tiled=True)


def on_device(
    activations, cotangent, kernel, channel_gain, master_flat, moment_mean, moment_square
):
    pre_grad, keep, give = pl.pallas_call(
        grads_kernel,
        out_shape=(
            shape((2 * IMG, CMID), bf16),
            shape((64, TILES, 4, CG), bf16),
            shape((64, TILES, 4, CG), bf16),
        ),
        in_specs=[VMEM] * 3,
        out_specs=(VMEM,) * 3,
        scratch_shapes=[
            pltpu.VMEM((2 * IMG, CMID), f32),
            pltpu.VMEM((3, 2 * IMG, CMID), bf16),
            pltpu.VMEM((2 * OUT, CMID), f32),
            pltpu.VMEM((9, CMID, CG), f32),
            pltpu.VMEM((BLOCKS * USED + 8, CG), f32),
        ],
        compiler_params=grant(20),
        name="grads",
    )(activations, cotangent, kernel)
    got = swap_cores(give)
    input_grad = pl.pallas_call(
        input_kernel,
        out_shape=shape((2, SIDE, SIDE, CMID), bf16),
        in_specs=[VMEM] * 2,
        out_specs=VMEM,
        scratch_shapes=[pltpu.VMEM((3, 2 * IMG, CMID), bf16)],
        compiler_params=grant(12),
        name="input_grad",
    )(pre_grad, kernel)
    pair = (keep.astype(f32) + got.astype(f32)).astype(bf16)
    pair, input_grad = lax.optimization_barrier((pair, input_grad))
    parts = exchange(pair, ZY)
    payload = pl.pallas_call(
        reduce_kernel,
        out_shape=shape((4, 48, CG), f32),
        in_specs=[VMEM] * 4,
        out_specs=VMEM,
        compiler_params=grant(4),
        name="reduce",
    )(parts, moment_mean, moment_square, master_flat)
    gathered = exchange(payload, "x")
    grad, send = pl.pallas_call(
        adam_kernel,
        out_shape=(shape((ROWS, CG), f32), shape((64, TILES, 4, CG), bf16)),
        in_specs=[VMEM, VMEM],
        out_specs=(VMEM,) * 2,
        scratch_shapes=[pltpu.VMEM((3, 40, CG), f32)],
        compiler_params=grant(4),
        name="adam",
    )(gathered, channel_gain.reshape(3, CG))
    own = exchange(send, ZY)
    other = swap_cores(own)
    grad_shard = lax.dynamic_slice(
        grad.reshape(ROWS * CG), (lax.axis_index("x") * SHARD,), (SHARD,)
    )
    mean_next, square_next, master_next = adam(
        moment_mean, moment_square, master_flat, grad_shard
    )
    kernel_next = pl.pallas_call(
        assemble_kernel,
        out_shape=shape((CMID, FAN), bf16),
        in_specs=[VMEM] * 2,
        out_specs=pl.BlockSpec(memory_space=pl.ANY),
        scratch_shapes=[
            pltpu.VMEM((BLOCKS * USED + 8, CG), f32),
            pltpu.VMEM((9, CMID, CG), f32),
            pltpu.VMEM((3, CMID, 3 * CG), bf16),
            pltpu.SemaphoreType.DMA((3,)),
        ],
        compiler_params=grant(10),
        name="assemble",
    )(own, other)
    return (input_grad, master_next, mean_next, square_next, kernel_next)


def solution(mesh):
    fine = Mesh(mesh.devices.reshape(SIZES), AXES)
    images = P(AXES, None, None, None)
    state = P(AXES)
    return jax.shard_map(
        on_device,
        mesh=fine,
        in_specs=(images, images, P(), P(), state, state, state),
        out_specs=(images, state, state, state, P()),
        check_vma=False,
    )
```
